256 devices in a mesh: req: 16 (over y, x_hi, core), tp: 16 (over x_lo, z).
Axes of the slice: x: 4 (x_hi: 2, x_lo: 2; x = x_hi * 2 + x_lo), y: 4, z: 8, core: 2. Of those that a mesh axis runs over, the one named last changes fastest.
Arguments:
- patches: bfloat16 [16, 1024, 1664], P('req', 'tp'), may hold values from -6 to 6
- vis_gain: float32 [1664], replicated, may hold values from 0.1 to 1.9
- w_fc1: bfloat16 [1664, 8192], P(None, 'tp'), may hold values from -0.15625 to 0.15625
- w_fc2: bfloat16 [8192, 1664], P('tp'), may hold values from -0.125 to 0.125
- merge_gain: float32 [1664], replicated, may hold values from 0.1 to 1.9
- w_merge: bfloat16 [6656, 1664], P('tp'), may hold values from -0.078125 to 0.078125
- slots: int32 [16, 256], P('req'), may hold values from 0 to 3071, as said below
- text: bfloat16 [16, 3072, 1664], P('req', 'tp'), may hold values from -6 to 6
- docs: int32 [16, 3072], P('req'), may hold values from 0 to 7, never falling along the last dimension, each value on 1 to 768 neighbouring positions
- dec_gain: float32 [1664], replicated, may hold values from 0.1 to 1.9
- w_qkv: bfloat16 [1664, 4992], P(None, 'tp'), may hold values from -0.2773501 to 0.2773501
- w_out: bfloat16 [1664, 1664], P('tp'), may hold values from -0.625 to 0.625
Outputs:
- decoded: bfloat16 [16, 3072, 1664], P('req', 'tp')
The draws below stay inside these ranges and needn't reach their ends.
Inputs may be any that keep to these rules, and one draw needn't show every extreme that they name: `slots`: positions in a group are distinct; each image's 64 merged rows take consecutive positions in order, and image k lies within positions j * 768 to (j + 1) * 768 - 1 with j = (k + 2) mod 4; the image with j = 3 takes the last 64 positions of the prompt. `docs`: request numbers never fall along a prompt; each request spans 1 to 768 positions.
All inputs are finite; a program needn't handle non-finite values.
Results may differ from the reference program's by a relative error of at most 0.033.
Values may be sent and summed in bfloat16 or wider, within the bound.
A program may use at most 64 MiB of HBM per device.

```python
import math
import jax
import jax.numpy as jnp
import numpy as np
from jax import lax

VD = 1664
FF = 8192
D = 1664
HEADS = 16
HD = 104
IMG_ROWS = 64
DOCS = 8
GROUPS = 16
PATCH = 1024
MGRP = 256
SEQ = 3072
IMAGES = 4
N_TP = 16


def draw_slots(key, part):
    span = SEQ // IMAGES
    image_ids = jnp.arange(IMAGES, dtype=jnp.int32)
    target = (image_ids + IMAGES // 2) % IMAGES
    random_starts = jax.random.randint(key, (GROUPS, IMAGES), 0, span - IMG_ROWS + 1)
    final_span = (target == IMAGES - 1)[None, :]
    starts = jnp.where(final_span, span - IMG_ROWS, random_starts) + target[None, :] * span
    rows = starts[:, :, None] + jnp.arange(IMG_ROWS, dtype=jnp.int32)[None, None, :]
    return rows.reshape(GROUPS, MGRP).astype(jnp.int32)


def draw_text(key, part):
    values = jax.random.truncated_normal(jax.random.fold_in(key, 21), -6.0, 6.0, (GROUPS, SEQ, D), jnp.float32)
    return values.astype(jnp.bfloat16)


def draw_w_qkv(key, part):
    spread = (D // 2) ** (-0.5)
    values = jax.random.truncated_normal(jax.random.fold_in(key, 31), -6.0, 6.0, (D, 3 * D), jnp.float32) * spread
    return values.astype(jnp.bfloat16)


def levels(rng, shape, shards, smallest, high):
    level, own = 1.0, jax.random.fold_in(rng, 6)
    for dim, blocks in shards:
        heights = jnp.exp(jax.random.uniform(jax.random.fold_in(own, dim), (blocks,), jnp.float32, smallest / len(shards), high / len(shards)))
        level = level * jnp.repeat(heights, shape[dim] // blocks).reshape([-1 if axis == dim else 1 for axis in range(len(shape))])
    return level


def profile(count, total, bound, slope):
    portions = [(1 << 20) // math.isqrt(rank ** slope) + 1 for rank in range(2, count + 1)]
    rest, given = total - bound - (count - 1), [1] * (count - 1)
    while rest > 0:
        candidates = [i for i in range(count - 1) if given[i] < bound]
        whole, left = sum([portions[i] for i in candidates]), rest
        for i in candidates:
            extra = min(bound - given[i], max(1, left * portions[i] // whole), rest)
            given[i] = given[i] + extra
            rest = rest - extra
    return np.array([bound] + given)


def uneven(rng, count, total, reach, lean):
    if count == 2:
        one = jax.random.randint(rng, (), max(1, total - reach), min(reach, total - 1) + 1)
        return jnp.stack([one, total - one])
    lengths = jnp.asarray(profile(count, total, reach, lean), jnp.int32)
    couples = (count - 1) // 2
    giver, receiver = lengths[1:1 + 2 * couples:2], lengths[2:2 + 2 * couples:2]
    margin = jnp.minimum(giver - 1, reach - receiver)
    moved = jax.random.randint(jax.random.fold_in(rng, 1), (couples,), 0, 1 << 20) % (margin + 1)
    lengths = lengths.at[1:1 + 2 * couples:2].set(giver - moved).at[2:2 + 2 * couples:2].set(receiver + moved)
    return lengths[jax.random.permutation(jax.random.fold_in(rng, 2), count)]


def bell_draw(stream_key, extent, deviation, bound, shards=(), held_as=jnp.bfloat16):
    entries = jax.random.normal(stream_key, extent, jnp.float32) * deviation
    if len(shards) > 0:
        entries = levels(stream_key, extent, shards, -0.22, 0.18) * entries
    return jnp.clip(entries, min=-bound, max=bound).astype(held_as)


def setup_inputs(seed: int = 0) -> dict:
    streams_of = jax.random.split(jax.random.key(seed), 13)
    return {
        "patches": bell_draw(streams_of[0], (GROUPS, PATCH, VD), 1.0, 6.0, ((0, 16), (1, 16))),
        "vis_gain": jnp.clip(1.0 + 0.18 * jax.random.normal(streams_of[1], (VD,), jnp.float32), 0.1, 1.9),
        "w_fc1": bell_draw(streams_of[2], (VD, FF), VD ** -0.5, 0.15625, ((1, 16),)),
        "w_fc2": bell_draw(streams_of[3], (FF, VD), (FF // 4) ** -0.5, 0.125, ((0, 16),)),
        "merge_gain": jnp.clip(1.0 + 0.18 * jax.random.normal(streams_of[4], (VD,), jnp.float32), 0.1, 1.9),
        "w_merge": bell_draw(streams_of[5], (4 * VD, D), (4 * VD) ** -0.5, 0.078125, ((0, 16),)),
        "slots": draw_slots(jax.random.fold_in(streams_of[12], 71), 0),
        "text": draw_text(jax.random.fold_in(streams_of[12], 71), 0),
        "docs": jax.vmap(lambda own: jnp.searchsorted(jnp.cumsum(uneven(own, DOCS, SEQ, SEQ // 4, 2)), jnp.arange(SEQ), side="right"))(jax.random.split(streams_of[8], GROUPS)).reshape((GROUPS, SEQ)).astype(jnp.int32),
        "dec_gain": jnp.clip(1.0 + 0.18 * jax.random.normal(streams_of[9], (D,), jnp.float32), 0.1, 1.9),
        "w_qkv": draw_w_qkv(jax.random.fold_in(streams_of[12], 71), 0),
        "w_out": bell_draw(streams_of[11], (D, D), HD ** -0.5, 0.625, ((0, 16),)),
    }


EPSILON = 1e-06

def layer_norm(values, gains):
    average = lax.optimization_barrier(jnp.mean(values, axis=-1, keepdims=True))
    centred = values - average
    variance = lax.optimization_barrier(jnp.mean(centred * centred, axis=-1, keepdims=True))
    return centred * lax.rsqrt(variance + EPSILON) * gains

def rms_norm(values, gains):
    return values * lax.rsqrt(lax.optimization_barrier(jnp.mean(values * values, axis=-1, keepdims=True)) + EPSILON) * gains

def rounded_sum(parts):
    narrow = lax.optimization_barrier(parts.astype(jnp.bfloat16))
    return lax.optimization_barrier(jnp.sum(narrow.astype(jnp.float32), axis=0))

def reference(patches, vis_gain, w_fc1, w_fc2, merge_gain, w_merge, slots, text, docs, dec_gain, w_qkv, w_out):
    block_rows = min(512, SEQ)

    def one_group(packed):
        patch_rows, slot_row, text_rows, doc_row = packed
        wide_in = patch_rows.astype(jnp.float32)
        normed_in = layer_norm(wide_in, vis_gain.astype(jnp.float32)).astype(jnp.bfloat16)
        hidden = jax.nn.gelu(jnp.dot(normed_in, w_fc1, preferred_element_type=jnp.float32), approximate=False).astype(jnp.bfloat16)
        mlp_parts = jnp.einsum('pjh,jhv->jpv', hidden.reshape(PATCH, N_TP, FF // N_TP).astype(jnp.float32), w_fc2.reshape(N_TP, FF // N_TP, VD).astype(jnp.float32))
        mlp_sum = rounded_sum(mlp_parts)
        normed_out = layer_norm(wide_in + mlp_sum, merge_gain.astype(jnp.float32)).astype(jnp.bfloat16)
        merge_in = normed_out.reshape(MGRP, 4 * VD)
        merge_parts = jnp.einsum('mjf,jfd->jmd', merge_in.reshape(MGRP, N_TP, 4 * VD // N_TP).astype(jnp.float32), w_merge.reshape(N_TP, 4 * VD // N_TP, D).astype(jnp.float32))
        merged = rounded_sum(merge_parts).astype(jnp.bfloat16)
        embedded = text_rows.at[slot_row].set(merged)
        dec_in = rms_norm(embedded.astype(jnp.float32), dec_gain.astype(jnp.float32)).astype(jnp.bfloat16)
        qkv = jnp.dot(dec_in, w_qkv, preferred_element_type=jnp.float32).astype(jnp.bfloat16)
        shaped = qkv.reshape(SEQ, HEADS, 3, HD).astype(jnp.float32)
        queries = shaped[:, :, 0]
        key_rows = shaped[:, :, 1]
        value_rows = shaped[:, :, 2]
        key_pos = jnp.arange(SEQ)

        def one_block(block_index):
            offset = block_index * block_rows
            query_block = lax.dynamic_slice_in_dim(queries, offset, block_rows, 0)
            query_pos = offset + jnp.arange(block_rows)
            query_docs = lax.dynamic_slice_in_dim(doc_row, offset, block_rows, 0)
            scores = jnp.einsum('qhe,khe->hqk', query_block, key_rows) / math.sqrt(HD)
            allowed = (key_pos[None, :] <= query_pos[:, None]) & (doc_row[None, :] == query_docs[:, None])
            scores = jnp.where(allowed[None], scores, -1e+30)
            largest = lax.optimization_barrier(jnp.max(scores, axis=-1, keepdims=True))
            raised = jnp.where(allowed[None], jnp.exp(scores - largest), 0.0)
            weights = (raised / lax.optimization_barrier(jnp.sum(raised, axis=-1, keepdims=True))).astype(jnp.bfloat16)
            blended = jnp.einsum('hqk,khe->qhe', weights.astype(jnp.float32), value_rows)
            return blended.astype(jnp.bfloat16).reshape(block_rows, D)
        attended = lax.map(one_block, jnp.arange(SEQ // block_rows)).reshape(SEQ, D)
        out_parts = jnp.einsum('sjc,jcd->jsd', attended.reshape(SEQ, N_TP, D // N_TP).astype(jnp.float32), w_out.reshape(N_TP, D // N_TP, D).astype(jnp.float32))
        out_sum = rounded_sum(out_parts)
        return (embedded.astype(jnp.float32) + out_sum).astype(jnp.bfloat16)
    return lax.map(one_group, (patches, slots, text, docs))
```

```python
import functools
import math

import jax
import jax.numpy as jnp
from jax import lax
from jax.experimental import pallas as pl
from jax.experimental.pallas import tpu as pltpu
from jax.sharding import PartitionSpec as P

HD = 104
EPSILON = 1e-06
MESH = pl.DeviceIdType.MESH
RING = 8


def layer_norm(values, gains):
    average = jnp.mean(values, axis=-1, keepdims=True)
    centred = values - average
    variance = jnp.mean(centred * centred, axis=-1, keepdims=True)
    return centred * lax.rsqrt(variance + EPSILON) * gains


def rms_norm(values, gains):
    return values * lax.rsqrt(jnp.mean(values * values, axis=-1, keepdims=True) + EPSILON) * gains


def gelu(v):
    return 0.5 * v * (1.0 + lax.erf(v * math.sqrt(0.5)))


def slot_of(rel):
    if rel == 0:
        return 0
    if abs(rel) == 4:
        return 1
    return 2 * abs(rel) + (1 if rel > 0 else 0)


def vision_kernel(
    patch_ref, vg_ref, mg_ref, w1_hbm, w2_hbm, wm_hbm, out_ref,
    xg, acc, w1, w2, wm, rs_out, rs_in, fsend, frx, psend, prx, mg,
    local_sem, ws_sem, wr_sem, fs_sem, fr_sem, as_sem, ar_sem, rs_sem, rr_sem,
    ts_sem, tr_sem, ps_sem, pr_sem, gs_sem, gr_sem, xs_sem, xr_sem,
):
    r = lax.axis_index("req")
    t = lax.axis_index("tp")
    z = lax.rem(t, RING)
    xl = t // RING
    core = lax.rem(r, 2)
    xhi = lax.rem(r // 2, 2)
    inner = (r, (1 - xl) * RING + z)
    outer = (r + 2 - 4 * xhi, (1 - xl) * RING + z)
    sibling = (r + 1 - 2 * core, t)

    def column(k):
        return (r, xl * RING + lax.rem(z + k + RING, RING))

    rows = patch_ref.shape[0]
    half = rows // 2

    def remote(src, dst, ssem, rsem, dev):
        return pltpu.make_async_remote_copy(
            src_ref=src, dst_ref=dst, send_sem=ssem, recv_sem=rsem, device_id=dev, device_id_type=MESH
        )

    pending = []

    def send(src, dst, ssem, rsem, dev):
        c = remote(src, dst, ssem, rsem, dev)
        c.start()
        pending.append(c)
        return c

    barrier = pltpu.get_barrier_semaphore()
    peers = [column(k) for k in range(1, RING)] + [inner, outer, sibling]
    for dev in peers:
        pl.semaphore_signal(barrier, inc=1, device_id=dev, device_id_type=MESH)

    loads = [
        pltpu.make_async_copy(w1_hbm, w1.at[0], local_sem.at[0]),
        pltpu.make_async_copy(w2_hbm, w2.at[0], local_sem.at[1]),
        pltpu.make_async_copy(wm_hbm, wm.at[xl], local_sem.at[2]),
    ]
    for c in loads:
        c.start()

    wide = patch_ref[...].astype(jnp.float32)
    xg[0] = layer_norm(wide, vg_ref[...]).astype(jnp.bfloat16)
    pl.semaphore_wait(barrier, len(peers))

    ag = {}
    for d, s in ((0, 1), (1, -1)):
        ag[d, 0] = send(xg.at[0], xg.at[slot_of(-s)], as_sem.at[d, 0], ar_sem.at[d, 0], column(s))

    n1 = w1_hbm.shape[0] // 4
    n2 = w2_hbm.shape[0] // 4
    nm = wm_hbm.shape[0] // 2
    wx = []
    for i, dev in ((0, inner), (1, outer)):
        q = core * 2 + i
        a1 = pl.ds(pl.multiple_of(q * n1, 16), n1)
        a2 = pl.ds(pl.multiple_of(q * n2, 16), n2)
        wx.append((send(w1_hbm.at[a1], w1.at[1, a1], ws_sem.at[2 * i], wr_sem.at[2 * i], dev), w1.at[1, a1]))
        wx.append((send(w2_hbm.at[a2], w2.at[1, a2], ws_sem.at[2 * i + 1], wr_sem.at[2 * i + 1], dev), w2.at[1, a2]))
    am = pl.ds(pl.multiple_of(core * nm, 16), nm)
    wx.append((send(wm_hbm.at[am], wm.at[xl, am], ws_sem.at[4], wr_sem.at[4], inner), wm.at[1 - xl, am]))

    def mlp(pair, which):
        x = xg[2 * pair:2 * pair + 2].reshape(2 * rows, xg.shape[2])
        h = gelu(jnp.dot(x, w1[which], preferred_element_type=jnp.float32)).astype(jnp.bfloat16)
        return jnp.dot(h, w2[which], preferred_element_type=jnp.float32).reshape(2, rows, w2.shape[2])

    for step in range(4):
        for d, s in ((0, 1), (1, -1)):
            rel = -s * (step + 1)
            ag[d, step].wait_recv()
            if step < 3:
                src, dst = xg.at[slot_of(rel)], xg.at[slot_of(rel - s)]
                if step == 2:
                    part = pl.ds(d * half, half)
                    src, dst = src.at[part], dst.at[part]
                ag[d, step + 1] = send(src, dst, as_sem.at[d, step + 1], ar_sem.at[d, step + 1], column(s))
        if step == 0:
            loads[0].wait()
            loads[1].wait()
        pair = (step + 1) % 4
        acc[2 * pair:2 * pair + 2] = mlp(pair, 0)

    fwd = []
    for i, (c, ref) in enumerate(wx):
        c.wait_recv()
        fwd.append(send(ref, ref, fs_sem.at[i], fr_sem.at[i], sibling))
    for c in fwd[:4]:
        c.wait_recv()

    rs = {}
    for step in range(4):
        pair = (4 - step) % 4
        acc[2 * pair:2 * pair + 2] = acc[2 * pair:2 * pair + 2] + mlp(pair, 1)
        for d, s in ((0, 1), (1, -1)):
            block = acc.at[slot_of(s * (4 - step))]
            out = rs_out.at[d, step]
            if step == 0:
                part = pl.ds(d * half, half)
                out[part] = block[part].astype(jnp.bfloat16)
                rs[d, 0] = send(out.at[part], rs_in.at[d, 0, part], rs_sem.at[d, 0], rr_sem.at[d, 0], column(s))
                continue
            rs[d, step - 1].wait_recv()
            if step == 1:
                part = pl.ds(d * half, half)
                block[part] = block[part] + rs_in[d, 0, part].astype(jnp.float32)
                out[...] = block[...].astype(jnp.bfloat16)
            else:
                out[...] = (block[...] + rs_in[d, step - 1].astype(jnp.float32)).astype(jnp.bfloat16)
            rs[d, step] = send(out, rs_in.at[d, step], rs_sem.at[d, step], rr_sem.at[d, step], column(s))
    rs[0, 3].wait_recv()
    rs[1, 3].wait_recv()
    total = acc[0] + rs_in[0, 3].astype(jnp.float32) + rs_in[1, 3].astype(jnp.float32)
    nrm = layer_norm(patch_ref[...].astype(jnp.float32) + total, mg_ref[...]).astype(jnp.bfloat16)

    mrows = rows // 4
    width = wm_hbm.shape[0]
    to_row = lax.broadcasted_iota(jnp.int32, (rows, rows), 0)
    from_row = lax.broadcasted_iota(jnp.int32, (rows, rows), 1)
    order = (4 * (to_row % mrows) + to_row // mrows == from_row).astype(jnp.bfloat16)
    nrm = jnp.dot(order, nrm, preferred_element_type=jnp.float32).astype(jnp.bfloat16)
    for p in range(4):
        line = nrm[p * mrows:(p + 1) * mrows]
        for c in range(4):
            j = 4 * p + c
            fsend[j % RING, j // RING] = line[:, c * width:(c + 1) * width]
    a2a = []
    for k in range(1, RING):
        dest = lax.rem(z + k, RING)
        a2a.append(send(fsend.at[dest], frx.at[RING - k], ts_sem.at[k], tr_sem.at[k], column(k)))
    frx[0] = fsend[z]
    loads[2].wait()
    fwd[4].wait_recv()
    for c in a2a:
        c.wait_recv()

    part = jnp.dot(frx[:, 0].reshape(RING * mrows, width), wm[0], preferred_element_type=jnp.float32)
    part = part + jnp.dot(frx[:, 1].reshape(RING * mrows, width), wm[1], preferred_element_type=jnp.float32)
    psend[...] = part.reshape(psend.shape).astype(jnp.bfloat16)
    red = []
    for k in range(1, RING):
        red.append(send(psend.at[k], prx.at[RING - k], ps_sem.at[k], pr_sem.at[k], column(k)))
    total = part[:mrows]
    for c in red:
        c.wait_recv()
    for k in range(1, RING):
        total = total + prx[k].astype(jnp.float32)
    mg[t] = total.astype(jnp.bfloat16)

    gat, xfw = [], [send(mg.at[t], mg.at[t], xs_sem.at[0], xr_sem.at[0], inner)]
    for k in range(1, RING):
        gat.append(send(mg.at[t], mg.at[t], gs_sem.at[k], gr_sem.at[k], column(k)))
    for k in range(1, RING):
        src = xl * RING + lax.rem(z - k + RING, RING)
        gat[k - 1].wait_recv()
        xfw.append(send(mg.at[src], mg.at[src], xs_sem.at[k], xr_sem.at[k], inner))
    for c in xfw:
        c.wait_recv()
    out_ref[...] = mg[...].reshape(out_ref.shape)
    for c in pending:
        c.wait_send()


def vision(patches, vg, mgain, w1, w2, wm):
    rows, width = patches.shape
    hidden = w1.shape[1]
    mrows = rows // 4
    bf, f32 = jnp.bfloat16, jnp.float32
    dma = pltpu.SemaphoreType.DMA
    vmem = pl.BlockSpec(memory_space=pltpu.VMEM)
    hbm = pl.BlockSpec(memory_space=pl.ANY)
    return pl.pallas_call(
        vision_kernel,
        out_shape=jax.ShapeDtypeStruct((16 * mrows, width), bf),
        in_specs=[vmem] * 3 + [hbm] * 3,
        out_specs=vmem,
        scratch_shapes=[
            pltpu.VMEM((8, rows, width), bf),
            pltpu.VMEM((8, rows, width), f32),
            pltpu.VMEM((2, width, hidden), bf),
            pltpu.VMEM((2, hidden, width), bf),
            pltpu.VMEM((2, wm.shape[0], width), bf),
            pltpu.VMEM((2, 4, rows, width), bf),
            pltpu.VMEM((2, 4, rows, width), bf),
            pltpu.VMEM((8, 2, mrows, wm.shape[0]), bf),
            pltpu.VMEM((8, 2, mrows, wm.shape[0]), bf),
            pltpu.VMEM((8, mrows, width), bf),
            pltpu.VMEM((8, mrows, width), bf),
            pltpu.VMEM((16, mrows, width), bf),
            dma((3,)), dma((5,)), dma((5,)), dma((5,)), dma((5,)),
            dma((2, 4)), dma((2, 4)), dma((2, 4)), dma((2, 4)),
            dma((8,)), dma((8,)), dma((8,)), dma((8,)), dma((8,)), dma((8,)), dma((8,)), dma((8,)),
        ],
        compiler_params=pltpu.CompilerParams(
            collective_id=0, has_side_effects=True, vmem_limit_bytes=44 * 2**20
        ),
        cost_estimate=pl.CostEstimate(flops=200_000_000_000, bytes_accessed=50_000_000, transcendentals=0),
        name="vision",
    )(patches, vg, mgain, w1, w2, wm)


def attend(qkv_rows, doc_row):
    seq_len = qkv_rows.shape[0]
    block_rows = 256
    band = 1024
    queries = qkv_rows[:, :HD]
    pad = jnp.zeros((band - block_rows, HD), qkv_rows.dtype)
    key_rows = jnp.concatenate([pad, qkv_rows[:, HD:2 * HD]], axis=0)
    value_rows = jnp.concatenate([pad, qkv_rows[:, 2 * HD:]], axis=0)
    docs_pad = jnp.concatenate([jnp.full((band - block_rows,), -1, doc_row.dtype), doc_row])
    outs = []
    for start in range(0, seq_len, block_rows):
        q = queries[start:start + block_rows]
        k = key_rows[start:start + band]
        v = value_rows[start:start + band]
        qpos = start + jnp.arange(block_rows)
        kpos = start - (band - block_rows) + jnp.arange(band)
        allowed = (kpos[None, :] <= qpos[:, None]) & (
            docs_pad[None, start:start + band] == doc_row[start:start + block_rows, None]
        )
        scores = jnp.einsum("qe,ke->qk", q, k, preferred_element_type=jnp.float32) / math.sqrt(HD)
        scores = jnp.where(allowed, scores, -1e30)
        largest = jnp.max(scores, axis=-1, keepdims=True)
        raised = jnp.where(allowed, jnp.exp(scores - largest), 0.0)
        weights = (raised / jnp.sum(raised, axis=-1, keepdims=True)).astype(jnp.bfloat16)
        outs.append(jnp.dot(weights, v, preferred_element_type=jnp.float32).astype(jnp.bfloat16))
    return jnp.concatenate(outs, axis=0)


def shards(
    patches, vis_gain, w_fc1, w_fc2, merge_gain, w_merge, slots, text, docs, dec_gain, w_qkv, w_out
):
    slot_row = slots[0]
    text_rows = text[0]
    doc_row = docs[0]
    seq_here = text_rows.shape[0]
    text_in = rms_norm(text_rows.astype(jnp.float32), dec_gain).astype(jnp.bfloat16)
    text_all = lax.all_gather(text_in, "tp", axis=0, tiled=True)
    merged = vision(patches[0], vis_gain[None], merge_gain[None], w_fc1, w_fc2, w_merge)
    image_in = rms_norm(merged.astype(jnp.float32), dec_gain).astype(jnp.bfloat16)
    rows_in = text_all
    span = merged.shape[0] // 4
    for k in range(4):
        rows_in = lax.dynamic_update_slice_in_dim(
            rows_in, image_in[k * span:(k + 1) * span], slot_row[k * span], 0
        )
    qkv_rows = jnp.dot(rows_in, w_qkv, preferred_element_type=jnp.float32).astype(jnp.bfloat16)
    attended = attend(qkv_rows, doc_row)
    out_sum = lax.psum_scatter(
        jnp.dot(attended, w_out, preferred_element_type=jnp.float32).astype(jnp.bfloat16),
        "tp",
        scatter_dimension=0,
        tiled=True,
    ).astype(jnp.float32)
    positions = lax.axis_index("tp") * seq_here + jnp.arange(seq_here, dtype=jnp.int32)
    matches = slot_row[None, :] == positions[:, None]
    placed = jnp.dot(
        matches.astype(jnp.bfloat16), merged, preferred_element_type=jnp.float32
    ).astype(jnp.bfloat16)
    embedded = jnp.where(jnp.any(matches, axis=1)[:, None], placed, text_rows)
    decoded = (embedded.astype(jnp.float32) + out_sum).astype(jnp.bfloat16)
    return decoded[None]


def solution(mesh):
    placed = (
        P("req", "tp", None),
        P(),
        P(None, "tp"),
        P("tp", None),
        P(),
        P("tp", None),
        P("req", None),
        P("req", "tp", None),
        P("req", None),
        P(),
        P(None, "tp"),
        P("tp", None),
    )
    return jax.shard_map(
        shards, mesh=mesh, in_specs=placed, out_specs=P("req", "tp", None), check_vma=False
    )
```

```python
import functools
import math

import jax
import jax.numpy as jnp
from jax import lax
from jax.experimental import pallas as pl
from jax.experimental.pallas import tpu as pltpu
from jax.sharding import PartitionSpec as P

HD = 104
EPSILON = 1e-06
MESH = pl.DeviceIdType.MESH
RING = 8


def layer_norm(values, gains):
    average = jnp.mean(values, axis=-1, keepdims=True)
    centred = values - average
    variance = jnp.mean(centred * centred, axis=-1, keepdims=True)
    return centred * lax.rsqrt(variance + EPSILON) * gains


def rms_norm(values, gains):
    return values * lax.rsqrt(jnp.mean(values * values, axis=-1, keepdims=True) + EPSILON) * gains


def gelu(v):
    return 0.5 * v * (1.0 + lax.erf(v * math.sqrt(0.5)))


def slot_of(rel):
    if rel == 0:
        return 0
    if abs(rel) == 4:
        return 1
    return 2 * abs(rel) + (1 if rel > 0 else 0)


def vision_kernel(
    patch_ref, vg_ref, mg_ref, text_ref, dg_ref, w1_hbm, w2_hbm, wm_hbm, wc_hbm,
    out_ref, win, wg,
    ti, xg, acc, w1, w2, wm, rs_out, rs_in, fsend, frx, psend, prx, mg,
    local_sem, ws_sem, wr_sem, fs_sem, fr_sem, as_sem, ar_sem, rs_sem, rr_sem,
    ts_sem, tr_sem, ps_sem, pr_sem, gs_sem, gr_sem, xs_sem, xr_sem,
    zs_sem, zr_sem, ys_sem, yr_sem, y2s_sem, y2r_sem, os_sem, or_sem, ss_sem, sr_sem, hs_sem, hr_sem,
):
    r = lax.axis_index("req")
    t = lax.axis_index("tp")
    z = lax.rem(t, RING)
    xl = t // RING
    core = lax.rem(r, 2)
    xhi = lax.rem(r // 2, 2)
    inner = (r, (1 - xl) * RING + z)
    outer = (r + 2 - 4 * xhi, (1 - xl) * RING + z)
    sibling = (r + 1 - 2 * core, t)

    tp_size = 2 * RING
    after, before = (r, lax.rem(t + 1, tp_size)), (r, lax.rem(t + tp_size - 1, tp_size))
    y_next, y_prev = (lax.rem(r + 4, 16), t), (lax.rem(r + 12, 16), t)

    def column(k):
        return (r, xl * RING + lax.rem(z + k + RING, RING))

    rows = patch_ref.shape[0]
    half = rows // 2

    def remote(src, dst, ssem, rsem, dev):
        return pltpu.make_async_remote_copy(
            src_ref=src, dst_ref=dst, send_sem=ssem, recv_sem=rsem, device_id=dev, device_id_type=MESH
        )

    pending = []

    def send(src, dst, ssem, rsem, dev):
        c = remote(src, dst, ssem, rsem, dev)
        c.start()
        pending.append(c)
        return c

    barrier = pltpu.get_barrier_semaphore()
    peers = [column(k) for k in range(1, RING)] + [inner, outer, sibling, after, before, y_next, y_prev]
    for dev in peers:
        pl.semaphore_signal(barrier, inc=1, device_id=dev, device_id_type=MESH)

    loads = [
        pltpu.make_async_copy(wc_hbm, wg.at[t], local_sem.at[3]),
        pltpu.make_async_copy(w1_hbm, w1.at[0], local_sem.at[0]),
        pltpu.make_async_copy(w2_hbm, w2.at[0], local_sem.at[1]),
        pltpu.make_async_copy(wm_hbm, wm.at[xl], local_sem.at[2]),
    ]
    for c in loads:
        c.start()

    wide = patch_ref[...].astype(jnp.float32)
    xg[0] = layer_norm(wide, vg_ref[...]).astype(jnp.bfloat16)
    pl.semaphore_wait(barrier, len(peers))

    ag = {}
    for d, s in ((0, 1), (1, -1)):
        ag[d, 0] = send(xg.at[0], xg.at[slot_of(-s)], as_sem.at[d, 0], ar_sem.at[d, 0], column(s))

    n1 = w1_hbm.shape[0] // 4
    n2 = w2_hbm.shape[0] // 4
    nm = wm_hbm.shape[0] // 2
    wx = []
    for i, dev in ((0, inner), (1, outer)):
        q = core * 2 + i
        a1 = pl.ds(pl.multiple_of(q * n1, 16), n1)
        a2 = pl.ds(pl.multiple_of(q * n2, 16), n2)
        wx.append((send(w1_hbm.at[a1], w1.at[1, a1], ws_sem.at[2 * i], wr_sem.at[2 * i], dev), w1.at[1, a1]))
        wx.append((send(w2_hbm.at[a2], w2.at[1, a2], ws_sem.at[2 * i + 1], wr_sem.at[2 * i + 1], dev), w2.at[1, a2]))
    am = pl.ds(pl.multiple_of(core * nm, 16), nm)
    wx.append((send(wm_hbm.at[am], wm.at[xl, am], ws_sem.at[4], wr_sem.at[4], inner), wm.at[1 - xl, am]))

    quarter = wc_hbm.shape[0] // 4
    y = r // 4
    s_w = 1 - 2 * core
    ahead = column(s_w)

    def quarter_at(k):
        return pl.ds(pl.multiple_of(lax.rem(y + k, 4) * quarter, 8), quarter)

    def shard_at(k):
        return xl * RING + lax.rem(z - s_w * (k + 1) + RING, RING)

    zc = [send(wc_hbm.at[quarter_at(0)], wg.at[t, quarter_at(0)], zs_sem.at[0], zr_sem.at[0], ahead)]
    yc, y2c, xc, sc, hc = {}, {}, {}, [], []

    def from_column(k):
        piece = wg.at[shard_at(k), quarter_at(0)]
        zc[k].wait_recv()
        if k < 3:
            zc.append(send(piece, piece, zs_sem.at[k + 1], zr_sem.at[k + 1], ahead))
        yc[k] = (
            send(piece, piece, ys_sem.at[k, 0], yr_sem.at[k, 0], y_next),
            send(piece, piece, ys_sem.at[k, 1], yr_sem.at[k, 1], y_prev),
        )

    def from_y(k):
        for c in yc[k]:
            c.wait_recv()
        piece = wg.at[shard_at(k), quarter_at(3 if k % 2 == 0 else 1)]
        y2c[k] = send(piece, piece, y2s_sem.at[k], y2r_sem.at[k], y_next if k % 2 == 0 else y_prev)

    def both_halves(ref, i):
        n = wc_hbm.shape[0] // 2
        return ref.at[pl.ds(i * n, n)]

    def to_x(k):
        y2c[k].wait_recv()
        if k == 3:
            loads[0].wait()
            idx = xl * RING + lax.rem(z + 4 - 4 * core, RING)
        else:
            idx = shard_at(k)
        xc[k] = [
            send(both_halves(wg.at[idx], i), both_halves(wg.at[idx], i), os_sem.at[k, i], or_sem.at[k, i], dev)
            for i, dev in ((0, inner), (1, outer))
        ]
        if k < 3:
            sc.append(send(wg.at[idx], wg.at[idx], ss_sem.at[k], sr_sem.at[k], sibling))

    def from_x(k):
        if k == 3:
            idx = lax.rem(z + 4 - 4 * core, RING)
        else:
            idx = lax.rem(z - s_w * (k + 1) + RING, RING)
        idx = (1 - xl) * RING + idx
        for c in xc[k]:
            c.wait_recv()
        sc.append(send(wg.at[idx], wg.at[idx], ss_sem.at[3 + k], sr_sem.at[3 + k], sibling))

    def window(k):
        if k == 0:
            hc.append(send(ti, win.at[1], hs_sem.at[0], hr_sem.at[0], after))
            return
        hc[k - 1].wait_recv()
        if k < 4:
            hc.append(send(win.at[k], win.at[k + 1], hs_sem.at[k], hr_sem.at[k], after))

    def mlp(pair, which):
        x = xg[2 * pair:2 * pair + 2].reshape(2 * rows, xg.shape[2])
        h = gelu(jnp.dot(x, w1[which], preferred_element_type=jnp.float32)).astype(jnp.bfloat16)
        return jnp.dot(h, w2[which], preferred_element_type=jnp.float32).reshape(2, rows, w2.shape[2])

    for step in range(4):
        for d, s in ((0, 1), (1, -1)):
            rel = -s * (step + 1)
            ag[d, step].wait_recv()
            if step < 3:
                src, dst = xg.at[slot_of(rel)], xg.at[slot_of(rel - s)]
                if step == 2:
                    part = pl.ds(d * half, half)
                    src, dst = src.at[part], dst.at[part]
                ag[d, step + 1] = send(src, dst, as_sem.at[d, step + 1], ar_sem.at[d, step + 1], column(s))
        if step == 0:
            loads[1].wait()
            loads[2].wait()
        pair = (step + 1) % 4
        acc[2 * pair:2 * pair + 2] = mlp(pair, 0)
        from_column(step)
        if step >= 1:
            from_y(step - 1)
        if step >= 2:
            to_x(step - 2)
    ti[...] = rms_norm(text_ref[...].astype(jnp.float32), dg_ref[...]).astype(jnp.bfloat16)
    own_window = pltpu.make_async_copy(ti, win.at[0], local_sem.at[4])
    own_window.start()
    window(0)

    fwd = []
    for i, (c, ref) in enumerate(wx):
        c.wait_recv()
        fwd.append(send(ref, ref, fs_sem.at[i], fr_sem.at[i], sibling))
    for c in fwd[:4]:
        c.wait_recv()

    rs = {}
    for step in range(4):
        pair = (4 - step) % 4
        acc[2 * pair:2 * pair + 2] = acc[2 * pair:2 * pair + 2] + mlp(pair, 1)
        for d, s in ((0, 1), (1, -1)):
            block = acc.at[slot_of(s * (4 - step))]
            out = rs_out.at[d, step]
            if step == 0:
                part = pl.ds(d * half, half)
                out[part] = block[part].astype(jnp.bfloat16)
                rs[d, 0] = send(out.at[part], rs_in.at[d, 0, part], rs_sem.at[d, 0], rr_sem.at[d, 0], column(s))
                continue
            rs[d, step - 1].wait_recv()
            if step == 1:
                part = pl.ds(d * half, half)
                block[part] = block[part] + rs_in[d, 0, part].astype(jnp.float32)
                out[...] = block[...].astype(jnp.bfloat16)
            else:
                out[...] = (block[...] + rs_in[d, step - 1].astype(jnp.float32)).astype(jnp.bfloat16)
            rs[d, step] = send(out, rs_in.at[d, step], rs_sem.at[d, step], rr_sem.at[d, step], column(s))
        if step == 0:
            from_y(3)
            to_x(2)
        if step == 1:
            to_x(3)
            from_x(0)
        if step == 2:
            window(1)
        if step == 3:
            from_x(1)
    rs[0, 3].wait_recv()
    rs[1, 3].wait_recv()
    total = acc[0] + rs_in[0, 3].astype(jnp.float32) + rs_in[1, 3].astype(jnp.float32)
    nrm = layer_norm(patch_ref[...].astype(jnp.float32) + total, mg_ref[...]).astype(jnp.bfloat16)

    mrows = rows // 4
    width = wm_hbm.shape[0]
    to_row = lax.broadcasted_iota(jnp.int32, (rows, rows), 0)
    from_row = lax.broadcasted_iota(jnp.int32, (rows, rows), 1)
    order = (4 * (to_row % mrows) + to_row // mrows == from_row).astype(jnp.bfloat16)
    nrm = jnp.dot(order, nrm, preferred_element_type=jnp.float32).astype(jnp.bfloat16)
    for p in range(4):
        line = nrm[p * mrows:(p + 1) * mrows]
        for c in range(4):
            j = 4 * p + c
            fsend[j % RING, j // RING] = line[:, c * width:(c + 1) * width]
    a2a = []
    for k in range(1, RING):
        dest = lax.rem(z + k, RING)
        a2a.append(send(fsend.at[dest], frx.at[RING - k], ts_sem.at[k], tr_sem.at[k], column(k)))
    frx[0] = fsend[z]
    window(2)
    loads[3].wait()
    fwd[4].wait_recv()
    for c in a2a:
        c.wait_recv()

    part = jnp.dot(frx[:, 0].reshape(RING * mrows, width), wm[0], preferred_element_type=jnp.float32)
    part = part + jnp.dot(frx[:, 1].reshape(RING * mrows, width), wm[1], preferred_element_type=jnp.float32)
    psend[...] = part.reshape(psend.shape).astype(jnp.bfloat16)
    red = []
    for k in range(1, RING):
        red.append(send(psend.at[k], prx.at[RING - k], ps_sem.at[k], pr_sem.at[k], column(k)))
    from_x(2)
    total = part[:mrows]
    for c in red:
        c.wait_recv()
    for k in range(1, RING):
        total = total + prx[k].astype(jnp.float32)
    mg[t] = total.astype(jnp.bfloat16)

    gat, xfw = [], [send(mg.at[t], mg.at[t], xs_sem.at[0], xr_sem.at[0], inner)]
    for k in range(1, RING):
        gat.append(send(mg.at[t], mg.at[t], gs_sem.at[k], gr_sem.at[k], column(k)))
    window(3)
    from_x(3)
    for k in range(1, RING):
        src = xl * RING + lax.rem(z - k + RING, RING)
        gat[k - 1].wait_recv()
        xfw.append(send(mg.at[src], mg.at[src], xs_sem.at[k], xr_sem.at[k], inner))
    for c in xfw:
        c.wait_recv()
    out_ref[...] = mg[...].reshape(out_ref.shape)
    window(4)
    own_window.wait()
    for c in sc:
        c.wait_recv()
    for c in pending:
        c.wait_send()


def vision(patches, vg, mgain, text, dgain, w1, w2, wm, wc):
    rows, width = patches.shape
    hidden = w1.shape[1]
    mrows = rows // 4
    bf, f32 = jnp.bfloat16, jnp.float32
    dma = pltpu.SemaphoreType.DMA
    vmem = pl.BlockSpec(memory_space=pltpu.VMEM)
    hbm = pl.BlockSpec(memory_space=pl.ANY)
    return pl.pallas_call(
        vision_kernel,
        out_shape=(
            jax.ShapeDtypeStruct((16 * mrows, width), bf),
            jax.ShapeDtypeStruct((5, text.shape[0], width), bf),
            jax.ShapeDtypeStruct((16, wc.shape[0], width), bf),
        ),
        in_specs=[vmem] * 5 + [hbm] * 4,
        out_specs=(vmem, hbm, hbm),
        scratch_shapes=[
            pltpu.VMEM(text.shape, bf),
            pltpu.VMEM((8, rows, width), bf),
            pltpu.VMEM((8, rows, width), f32),
            pltpu.VMEM((2, width, hidden), bf),
            pltpu.VMEM((2, hidden, width), bf),
            pltpu.VMEM((2, wm.shape[0], width), bf),
            pltpu.VMEM((2, 4, rows, width), bf),
            pltpu.VMEM((2, 4, rows, width), bf),
            pltpu.VMEM((8, 2, mrows, wm.shape[0]), bf),
            pltpu.VMEM((8, 2, mrows, wm.shape[0]), bf),
            pltpu.VMEM((8, mrows, width), bf),
            pltpu.VMEM((8, mrows, width), bf),
            pltpu.VMEM((16, mrows, width), bf),
            dma((5,)), dma((5,)), dma((5,)), dma((5,)), dma((5,)),
            dma((2, 4)), dma((2, 4)), dma((2, 4)), dma((2, 4)),
            dma((8,)), dma((8,)), dma((8,)), dma((8,)), dma((8,)), dma((8,)), dma((8,)), dma((8,)),
            dma((4,)), dma((4,)), dma((4, 2)), dma((4, 2)), dma((4,)), dma((4,)),
            dma((4, 2)), dma((4, 2)), dma((7,)), dma((7,)), dma((4,)), dma((4,)),
        ],
        compiler_params=pltpu.CompilerParams(
            collective_id=0, has_side_effects=True, vmem_limit_bytes=56 * 2**20
        ),
        cost_estimate=pl.CostEstimate(flops=100_000_000_000, bytes_accessed=50_000_000, transcendentals=0),
        name="vision",
    )(patches, vg, mgain, text, dgain, w1, w2, wm, wc)


NT = (((1,), (1,)), ((), ()))


def decode_kernel(
    win_ref, merged_ref, text_ref, gain_ref, slot_ref, kcol_ref, krow_ref, dcol_ref, drow_ref, w_ref, out_ref,
    x, acc, bias,
):
    bf, f32 = jnp.bfloat16, jnp.float32
    rows = text_ref.shape[0]
    block = w_ref.shape[0] // 2

    @pl.when(pl.program_id(0) == 0)
    def _():
        match = kcol_ref[...] == slot_ref[...]
        onehot = match.astype(f32)
        hit = jnp.max(onehot, axis=1, keepdims=True) > 0.0
        onehot = onehot.astype(bf)
        image = rms_norm(merged_ref[...].astype(f32), gain_ref[...]).astype(bf)
        placed = jnp.dot(onehot, image, preferred_element_type=f32)
        x[...] = jnp.where(hit, placed, win_ref[...].astype(f32)).astype(bf)
        placed = jnp.dot(onehot[:rows], merged_ref[...], preferred_element_type=f32)
        acc[...] = jnp.where(hit[:rows], placed, text_ref[...].astype(f32))
        allowed = (krow_ref[...] <= kcol_ref[:rows, :]) & (drow_ref[...] == dcol_ref[...])
        bias[...] = jnp.where(allowed, 0.0, -1e30)

    lane = lax.broadcasted_iota(jnp.int32, (rows, block), 1)
    kv = lax.dot_general(x[...], w_ref[:block], NT, preferred_element_type=f32).astype(bf)
    q = lax.dot_general(x[:rows], w_ref[block:], NT, preferred_element_type=f32)
    q = jnp.where(lane < HD, q, 0.0).astype(bf)
    scores = lax.dot_general(q, kv, NT, preferred_element_type=f32) * (1.0 / math.sqrt(HD)) + bias[...]
    raised = jnp.exp(scores - jnp.max(scores, axis=1, keepdims=True))
    total = jnp.sum(raised, axis=1, keepdims=True)
    mixed = jnp.dot(raised.astype(bf), kv, preferred_element_type=f32) / total
    mixed = jnp.where(lane < HD, 0.0, mixed).astype(bf)
    acc[...] += jnp.dot(mixed, w_ref[block:], preferred_element_type=f32)

    @pl.when(pl.program_id(0) == pl.num_programs(0) - 1)
    def _():
        out_ref[...] = acc[...].astype(bf)


def decode(win, merged, text, gain, slots, kcol, krow, dcol, drow, wg):
    heads, depth, width = wg.shape
    rows = text.shape[0]
    span = win.shape[0]

    def whole(a):
        return pl.BlockSpec(a.shape, lambda h: (0,) * a.ndim)

    args = (win, merged, text, gain, slots, kcol, krow, dcol, drow)
    return pl.pallas_call(
        decode_kernel,
        grid=(heads,),
        out_shape=jax.ShapeDtypeStruct((rows, width), jnp.bfloat16),
        in_specs=[whole(a) for a in args] + [pl.BlockSpec((None, depth, width), lambda h: (h, 0, 0))],
        out_specs=pl.BlockSpec((rows, width), lambda h: (0, 0)),
        scratch_shapes=[
            pltpu.VMEM((span, width), jnp.bfloat16),
            pltpu.VMEM((rows, width), jnp.float32),
            pltpu.VMEM((rows, span), jnp.float32),
        ],
        compiler_params=pltpu.CompilerParams(vmem_limit_bytes=50 * 2**20),
        name="decode",
    )(*args, wg)


def shards(
    patches, vis_gain, w_fc1, w_fc2, merge_gain, w_merge, slots, text, docs, dec_gain, w_qkv, w_out
):
    text_rows = text[0]
    rows = text_rows.shape[0]
    across = w_qkv.T
    wc = jnp.concatenate([across[HD:], across[:HD], w_out], axis=0)
    merged, win, wg = vision(
        patches[0], vis_gain[None], merge_gain[None], text_rows, dec_gain[None], w_fc1, w_fc2, w_merge, wc
    )
    t = lax.axis_index("tp")
    doc_pad = jnp.concatenate([jnp.full((4 * rows,), -1, jnp.int32), docs[0]])
    doc_win = lax.dynamic_slice_in_dim(doc_pad, t * rows, 5 * rows, 0).reshape(5, rows)[::-1].reshape(-1)
    pos = ((t - jnp.arange(5, dtype=jnp.int32))[:, None] * rows + jnp.arange(rows, dtype=jnp.int32)).reshape(-1)
    out = decode(
        win.reshape(5 * rows, -1), merged, text_rows, dec_gain[None], slots,
        pos[:, None], pos[None], doc_win[:rows, None], doc_win[None], wg,
    )
    return out[None]


def solution(mesh):
    placed = (
        P("req", "tp", None),
        P(),
        P(None, "tp"),
        P("tp", None),
        P(),
        P("tp", None),
        P("req", None),
        P("req", "tp", None),
        P("req", None),
        P(),
        P(None, "tp"),
        P("tp", None),
    )
    return jax.shard_map(
        shards, mesh=mesh, in_specs=placed, out_specs=P("req", "tp", None), check_vma=False
    )
```

```python
import functools
import math

import jax
import jax.numpy as jnp
from jax import lax
from jax.experimental import pallas as pl
from jax.experimental.pallas import tpu as pltpu
from jax.sharding import PartitionSpec as P

HD = 104
EPSILON = 1e-06
MESH = pl.DeviceIdType.MESH
RING = 8


def layer_norm(values, gains):
    average = jnp.mean(values, axis=-1, keepdims=True)
    centred = values - average
    variance = jnp.mean(centred * centred, axis=-1, keepdims=True)
    return centred * lax.rsqrt(variance + EPSILON) * gains


def rms_norm(values, gains):
    return values * lax.rsqrt(jnp.mean(values * values, axis=-1, keepdims=True) + EPSILON) * gains


def gelu(v):
    return 0.5 * v * (1.0 + lax.erf(v * math.sqrt(0.5)))


def slot_of(rel):
    if rel == 0:
        return 0
    if abs(rel) == 4:
        return 1
    return 2 * abs(rel) + (1 if rel > 0 else 0)


def vision_kernel(
    patch_ref, text_ref, gain_ref, slot_ref, dcol_ref, drow_ref, w1_hbm, w2_hbm, wm_hbm, wc_hbm,
    out_ref,
    win, wg, bias, total, xg, acc, w1, w2, wm, rs_out, rs_in, fsend, frx, psend, prx, mg, mine,
    local_sem, ws_sem, wr_sem, fs_sem, fr_sem, as_sem, ar_sem, rs_sem, rr_sem,
    ts_sem, tr_sem, ps_sem, pr_sem, gs_sem, gr_sem,
    ms_sem, mr_sem, ns_sem, nr_sem, zs_sem, zr_sem, ys_sem, yr_sem, y2s_sem, y2r_sem, os_sem, or_sem, ss_sem, sr_sem, hs_sem, hr_sem,
):
    r = lax.axis_index("req")
    t = lax.axis_index("tp")
    z = lax.rem(t, RING)
    xl = t // RING
    core = lax.rem(r, 2)
    xhi = lax.rem(r // 2, 2)
    inner = (r, (1 - xl) * RING + z)
    outer = (r + 2 - 4 * xhi, (1 - xl) * RING + z)
    sibling = (r + 1 - 2 * core, t)

    tp_size = 2 * RING
    after = (r, lax.rem(t + 1, tp_size))
    y_next, y_prev = (lax.rem(r + 4, 16), t), (lax.rem(r + 12, 16), t)

    def column(k):
        return (r, xl * RING + lax.rem(z + k + RING, RING))

    rows = patch_ref.shape[0]
    half = rows // 2

    def remote(src, dst, ssem, rsem, dev):
        return pltpu.make_async_remote_copy(
            src_ref=src, dst_ref=dst, send_sem=ssem, recv_sem=rsem, device_id=dev, device_id_type=MESH
        )

    pending = []

    def send(src, dst, ssem, rsem, dev):
        c = remote(src, dst, ssem, rsem, dev)
        c.start()
        pending.append(c)
        return c

    barrier = pltpu.get_barrier_semaphore()
    peers = [(r, lax.rem(t + k, tp_size)) for k in range(1, tp_size)] + [outer, sibling, y_next, y_prev]
    for dev in peers:
        pl.semaphore_signal(barrier, inc=1, device_id=dev, device_id_type=MESH)

    loads = [
        pltpu.make_async_copy(wc_hbm, wg.at[t], local_sem.at[3]),
        pltpu.make_async_copy(w1_hbm, w1.at[0], local_sem.at[0]),
        pltpu.make_async_copy(w2_hbm, w2.at[0], local_sem.at[1]),
        pltpu.make_async_copy(wm_hbm, wm.at[xl], local_sem.at[2]),
    ]
    for c in loads:
        c.start()

    wide = patch_ref[...].astype(jnp.float32)
    xg[0] = layer_norm(wide, gain_ref[0:1]).astype(jnp.bfloat16)
    pl.semaphore_wait(barrier, len(peers))

    ag = {}
    for d, s in ((0, 1), (1, -1)):
        ag[d, 0] = send(xg.at[0], xg.at[slot_of(-s)], as_sem.at[d, 0], ar_sem.at[d, 0], column(s))

    n1 = w1_hbm.shape[0] // 4
    n2 = w2_hbm.shape[0] // 4
    wx = []
    for i, dev in ((0, inner), (1, outer)):
        q = core * 2 + i
        a1 = pl.ds(pl.multiple_of(q * n1, 16), n1)
        a2 = pl.ds(pl.multiple_of(q * n2, 16), n2)
        wx.append((send(w1_hbm.at[a1], w1.at[1, a1], ws_sem.at[2 * i], wr_sem.at[2 * i], dev), w1.at[1, a1]))
        wx.append((send(w2_hbm.at[a2], w2.at[1, a2], ws_sem.at[2 * i + 1], wr_sem.at[2 * i + 1], dev), w2.at[1, a2]))
    quarter = wc_hbm.shape[0] // 4
    y = r // 4
    s_w = 1 - 2 * core
    ahead = column(s_w)

    def quarter_at(k):
        return pl.ds(pl.multiple_of(lax.rem(y + k, 4) * quarter, 16), quarter)

    def shard_at(k):
        return xl * RING + lax.rem(z - s_w * (k + 1) + RING, RING)

    mx = []

    def merge_weights():
        for i, dev in ((0, inner), (1, outer)):
            at = pl.ds(pl.multiple_of(core * 208 + 112 * i, 16), (112, 96)[i])
            mx.append((send(wm_hbm.at[at], wm.at[xl, at], ms_sem.at[i], mr_sem.at[i], dev), wm.at[1 - xl, at]))

    zc = [send(wc_hbm.at[quarter_at(0)], wg.at[t, quarter_at(0)], zs_sem.at[0], zr_sem.at[0], ahead)]
    yc, y2c, xc, sc, hc = {}, {}, {}, [], []

    def from_column(k):
        piece = wg.at[shard_at(k), quarter_at(0)]
        zc[k].wait_recv()
        if k < 3:
            zc.append(send(piece, piece, zs_sem.at[k + 1], zr_sem.at[k + 1], ahead))
        yc[k] = (
            send(piece, piece, ys_sem.at[k, 0], yr_sem.at[k, 0], y_next),
            send(piece, piece, ys_sem.at[k, 1], yr_sem.at[k, 1], y_prev),
        )

    def from_y(k):
        for c in yc[k]:
            c.wait_recv()
        piece = wg.at[shard_at(k), quarter_at(3 if k % 2 == 0 else 1)]
        y2c[k] = send(piece, piece, y2s_sem.at[k], y2r_sem.at[k], y_next if k % 2 == 0 else y_prev)

    def both_halves(ref, i):
        n = wc_hbm.shape[0] // 2
        return ref.at[pl.ds(i * n, n)]

    def to_x(k):
        y2c[k].wait_recv()
        if k == 3:
            loads[0].wait()
            idx = xl * RING + lax.rem(z + 4 - 4 * core, RING)
        else:
            idx = shard_at(k)
        xc[k] = [
            send(both_halves(wg.at[idx], i), both_halves(wg.at[idx], i), os_sem.at[k, i], or_sem.at[k, i], dev)
            for i, dev in ((0, inner), (1, outer))
        ]
        if k < 3:
            sc.append(send(wg.at[idx], wg.at[idx], ss_sem.at[k], sr_sem.at[k], sibling))

    def from_x(k):
        if k == 3:
            idx = lax.rem(z + 4 - 4 * core, RING)
        else:
            idx = lax.rem(z - s_w * (k + 1) + RING, RING)
        idx = (1 - xl) * RING + idx
        for c in xc[k]:
            c.wait_recv()
        sc.append(send(wg.at[idx], wg.at[idx], ss_sem.at[3 + k], sr_sem.at[3 + k], sibling))

    def window(k):
        if k == 0:
            hc.append(send(win.at[0], win.at[1], hs_sem.at[0], hr_sem.at[0], after))
            return
        hc[k - 1].wait_recv()
        if k < 4:
            hc.append(send(win.at[k], win.at[k + 1], hs_sem.at[k], hr_sem.at[k], after))

    def mlp(pair, which):
        x = xg[2 * pair:2 * pair + 2].reshape(2 * rows, xg.shape[2])
        h = gelu(jnp.dot(x, w1[which], preferred_element_type=jnp.float32)).astype(jnp.bfloat16)
        return jnp.dot(h, w2[which], preferred_element_type=jnp.float32).reshape(2, rows, w2.shape[2])

    for step in range(4):
        for d, s in ((0, 1), (1, -1)):
            rel = -s * (step + 1)
            ag[d, step].wait_recv()
            if step < 3:
                src, dst = xg.at[slot_of(rel)], xg.at[slot_of(rel - s)]
                if step == 2:
                    part = pl.ds(d * half, half)
                    src, dst = src.at[part], dst.at[part]
                ag[d, step + 1] = send(src, dst, as_sem.at[d, step + 1], ar_sem.at[d, step + 1], column(s))
        if step == 0:
            loads[1].wait()
            loads[2].wait()
        pair = (step + 1) % 4
        acc[2 * pair:2 * pair + 2] = mlp(pair, 0)
        from_column(step)
        if step >= 1:
            from_y(step - 1)
        if step >= 2:
            to_x(step - 2)
        if step == 1:
            win[0] = rms_norm(text_ref[...].astype(jnp.float32), gain_ref[2:3]).astype(jnp.bfloat16)
    window(0)

    fwd = []
    for i, (c, ref) in enumerate(wx):
        c.wait_recv()
        fwd.append(send(ref, ref, fs_sem.at[i], fr_sem.at[i], sibling))
    merge_weights()
    for c in fwd:
        c.wait_recv()

    rs = {}
    for step in range(4):
        pair = (4 - step) % 4
        acc[2 * pair:2 * pair + 2] = acc[2 * pair:2 * pair + 2] + mlp(pair, 1)
        for d, s in ((0, 1), (1, -1)):
            block = acc.at[slot_of(s * (4 - step))]
            out = rs_out.at[d, step]
            if step == 0:
                part = pl.ds(d * half, half)
                out[part] = block[part].astype(jnp.bfloat16)
                rs[d, 0] = send(out.at[part], rs_in.at[d, 0, part], rs_sem.at[d, 0], rr_sem.at[d, 0], column(s))
                continue
            rs[d, step - 1].wait_recv()
            if step == 1:
                part = pl.ds(d * half, half)
                block[part] = block[part] + rs_in[d, 0, part].astype(jnp.float32)
                out[...] = block[...].astype(jnp.bfloat16)
            else:
                out[...] = (block[...] + rs_in[d, step - 1].astype(jnp.float32)).astype(jnp.bfloat16)
            rs[d, step] = send(out, rs_in.at[d, step], rs_sem.at[d, step], rr_sem.at[d, step], column(s))
        if step == 0:
            from_y(3)
            to_x(2)
        if step == 1:
            to_x(3)
            mf = []
            for i, (c, ref) in enumerate(mx):
                c.wait_recv()
                mf.append(send(ref, ref, ns_sem.at[i], nr_sem.at[i], sibling))
        if step == 2:
            window(1)
            from_x(0)
        if step == 3:
            from_x(1)
    rs[0, 3].wait_recv()
    rs[1, 3].wait_recv()
    summed = acc[0] + rs_in[0, 3].astype(jnp.float32) + rs_in[1, 3].astype(jnp.float32)
    nrm = layer_norm(patch_ref[...].astype(jnp.float32) + summed, gain_ref[1:2]).astype(jnp.bfloat16)

    mrows = rows // 4
    width = wm_hbm.shape[0]
    to_row = lax.broadcasted_iota(jnp.int32, (rows, rows), 0)
    from_row = lax.broadcasted_iota(jnp.int32, (rows, rows), 1)
    order = (4 * (to_row % mrows) + to_row // mrows == from_row).astype(jnp.bfloat16)
    nrm = jnp.dot(order, nrm, preferred_element_type=jnp.float32).astype(jnp.bfloat16)
    for p in range(4):
        line = nrm[p * mrows:(p + 1) * mrows]
        for c in range(4):
            j = 4 * p + c
            fsend[j % RING, j // RING] = line[:, c * width:(c + 1) * width]
    a2a = []
    for k in range(1, RING):
        dest = lax.rem(z + k, RING)
        a2a.append(send(fsend.at[dest], frx.at[RING - k], ts_sem.at[k], tr_sem.at[k], column(k)))
    frx[0] = fsend[z]
    window(2)
    loads[3].wait()
    for c in mf:
        c.wait_recv()
    for c in a2a:
        c.wait_recv()

    part = jnp.dot(frx[:, 0].reshape(RING * mrows, width), wm[0], preferred_element_type=jnp.float32)
    part = part + jnp.dot(frx[:, 1].reshape(RING * mrows, width), wm[1], preferred_element_type=jnp.float32)
    psend[...] = part.reshape(psend.shape).astype(jnp.bfloat16)
    red = []
    for k in range(1, RING):
        red.append(send(psend.at[k], prx.at[RING - k], ps_sem.at[k], pr_sem.at[k], column(k)))
    from_x(2)
    summed = part[:mrows]
    for c in red:
        c.wait_recv()
    for k in range(1, RING):
        summed = summed + prx[k].astype(jnp.float32)
    mine[...] = summed.astype(jnp.bfloat16)

    quad, lane4 = t // 4, lax.rem(t, 4)
    gat = []
    for i in range(2):
        for k in range(4):
            dest = lax.rem(quad + 2 + i, 4) * 4 + lax.rem(lane4 + k, 4)
            gat.append(send(mine, mg.at[4 * i + lane4], gs_sem.at[4 * i + k], gr_sem.at[4 * i + k], (r, dest)))
    window(3)
    from_x(3)

    seq = text_ref.shape[0]
    depth = wc_hbm.shape[0] // 2
    lane = lax.broadcasted_iota(jnp.int32, (1, 5 * seq), 1)
    back = sum([(lane >= m * seq).astype(jnp.int32) for m in range(1, 5)])
    kpos = (t - 2 * back) * seq + lane
    qpos = t * seq + lax.broadcasted_iota(jnp.int32, (seq, 1), 0)
    allowed = (kpos <= qpos) & (drow_ref[...] == dcol_ref[...])
    bias[...] = jnp.where(allowed, 0.0, -1e30)
    window(4)
    for c in sc:
        c.wait_recv()
    for c in hc:
        c.wait_send()
    for c in gat:
        c.wait_recv()
    raw = mg[...].reshape(8 * mrows, mg.shape[2])
    image = rms_norm(raw.astype(jnp.float32), gain_ref[2:3]).astype(jnp.bfloat16)
    for k in range(5):
        pos = (t - k) * seq + lax.broadcasted_iota(jnp.int32, (seq, 1), 0)
        onehot = (pos == slot_ref[...]).astype(jnp.float32)
        hit = jnp.max(onehot, axis=1, keepdims=True) > 0.0
        onehot = onehot.astype(jnp.bfloat16)
        placed = jnp.dot(onehot, image, preferred_element_type=jnp.float32)
        win[k] = jnp.where(hit, placed, win[k].astype(jnp.float32)).astype(jnp.bfloat16)
        if k == 0:
            placed = jnp.dot(onehot, raw, preferred_element_type=jnp.float32)
            total[...] = jnp.where(hit, placed, text_ref[...].astype(jnp.float32))

    lane = lax.broadcasted_iota(jnp.int32, (seq, depth), 1)
    split = depth // 2

    def head(h):
        first, second = wg.at[h, :depth], wg.at[h, depth:]
        x = win[...].reshape(5 * seq, win.shape[2])
        kv = lax.dot_general(x, first[...], NT, preferred_element_type=jnp.float32).astype(jnp.bfloat16)
        q = lax.dot_general(win[0], second[...], NT, preferred_element_type=jnp.float32)
        q = jnp.where(lane < split, q, 0.0).astype(jnp.bfloat16)
        scores = lax.dot_general(q, kv, NT, preferred_element_type=jnp.float32) * (1.0 / math.sqrt(HD)) + bias[...]
        raised = jnp.exp(scores - jnp.max(scores, axis=1, keepdims=True))
        mass = jnp.sum(raised, axis=1, keepdims=True)
        mixed = jnp.dot(raised.astype(jnp.bfloat16), kv, preferred_element_type=jnp.float32) / mass
        mixed = jnp.where(lane < split, 0.0, mixed).astype(jnp.bfloat16)
        return jnp.dot(mixed, second[...], preferred_element_type=jnp.float32)

    def two_heads(i, carry):
        total[...] += head(2 * i) + head(2 * i + 1)
        return carry

    lax.fori_loop(0, wg.shape[0] // 2, two_heads, 0)
    out_ref[...] = total[...].astype(jnp.bfloat16)
    for c in pending:
        if not any(c is d for d in hc):
            c.wait_send()


NT = (((1,), (1,)), ((), ()))


def block(patches, text, gains, slots, dcol, drow, w1, w2, wm, wc):
    rows, width = patches.shape
    seq = text.shape[0]
    hidden = w1.shape[1]
    mrows = rows // 4
    bf, f32 = jnp.bfloat16, jnp.float32
    dma = pltpu.SemaphoreType.DMA
    vmem = pl.BlockSpec(memory_space=pltpu.VMEM)
    hbm = pl.BlockSpec(memory_space=pl.ANY)
    return pl.pallas_call(
        vision_kernel,
        out_shape=jax.ShapeDtypeStruct((seq, width), bf),
        in_specs=[vmem] * 6 + [hbm] * 4,
        out_specs=vmem,
        scratch_shapes=[
            pltpu.VMEM((5, seq, width), bf),
            pltpu.VMEM((16, wc.shape[0], width), bf),
            pltpu.VMEM((seq, 5 * seq), f32),
            pltpu.VMEM((seq, width), f32),
            pltpu.VMEM((8, rows, width), bf),
            pltpu.VMEM((8, rows, width), f32),
            pltpu.VMEM((2, width, hidden), bf),
            pltpu.VMEM((2, hidden, width), bf),
            pltpu.VMEM((2, wm.shape[0], width), bf),
            pltpu.VMEM((2, 4, rows, width), bf),
            pltpu.VMEM((2, 4, rows, width), bf),
            pltpu.VMEM((8, 2, mrows, wm.shape[0]), bf),
            pltpu.VMEM((8, 2, mrows, wm.shape[0]), bf),
            pltpu.VMEM((8, mrows, width), bf),
            pltpu.VMEM((8, mrows, width), bf),
            pltpu.VMEM((8, mrows, width), bf),
            pltpu.VMEM((mrows, width), bf),
            dma((4,)), dma((4,)), dma((4,)), dma((4,)), dma((4,)),
            dma((2, 4)), dma((2, 4)), dma((2, 4)), dma((2, 4)),
            dma((8,)), dma((8,)), dma((8,)), dma((8,)), dma((8,)), dma((8,)),
            dma((2,)), dma((2,)), dma((2,)), dma((2,)),
            dma((4,)), dma((4,)), dma((4, 2)), dma((4, 2)), dma((4,)), dma((4,)),
            dma((4, 2)), dma((4, 2)), dma((7,)), dma((7,)), dma((4,)), dma((4,)),
        ],
        compiler_params=pltpu.CompilerParams(
            collective_id=0, has_side_effects=True, vmem_limit_bytes=62 * 2**20
        ),
        name="block",
    )(patches, text, gains, slots, dcol, drow, w1, w2, wm, wc)


def shards(
    patches, vis_gain, w_fc1, w_fc2, merge_gain, w_merge, slots, text, docs, dec_gain, w_qkv, w_out
):
    text_rows = text[0]
    rows, width = text_rows.shape
    across = w_qkv.T
    gap = jnp.zeros((8, width), across.dtype)
    wc = jnp.concatenate(
        [across[HD:2 * HD], gap, across[2 * HD:], gap, across[:HD], gap, w_out, gap], axis=0
    )
    gains = jnp.stack([vis_gain, merge_gain, dec_gain])
    t = lax.axis_index("tp")
    doc_pad = jnp.concatenate([jnp.full((4 * rows,), -1, jnp.int32), docs[0]])
    doc_win = lax.dynamic_slice_in_dim(doc_pad, t * rows, 5 * rows, 0).reshape(5, rows)[::-1].reshape(-1)
    image_slots = slots[0].reshape(4, -1)
    quad = t // 4
    near = jnp.concatenate([
        lax.dynamic_index_in_dim(image_slots, lax.rem(quad + 2, 4), 0),
        lax.dynamic_index_in_dim(image_slots, lax.rem(quad + 1, 4), 0),
    ], axis=1)
    out = block(
        patches[0], text_rows, gains, near, doc_win[:rows, None], doc_win[None], w_fc1, w_fc2, w_merge, wc
    )
    return out[None]


def solution(mesh):
    placed = (
        P("req", "tp", None),
        P(),
        P(None, "tp"),
        P("tp", None),
        P(),
        P("tp", None),
        P("req", None),
        P("req", "tp", None),
        P("req", None),
        P(),
        P(None, "tp"),
        P("tp", None),
    )
    return jax.shard_map(
        shards, mesh=mesh, in_specs=placed, out_specs=P("req", "tp", None), check_vma=False
    )
```

```python
import functools
import math

import jax
import jax.numpy as jnp
from jax import lax
from jax.experimental import pallas as pl
from jax.experimental.pallas import tpu as pltpu
from jax.sharding import PartitionSpec as P

HD = 104
EPSILON = 1e-06
PLAN = {
    "A3": "z-1 h0", "R0": "z0", "R1": "z1", "R2": "z2 y0", "R3": "z3 h1", "L": "y1 x0", "T": "y2 x1 h2",
    "M": "y3 x2 h3", "G": "x3 h4", "D0": "f0 h5", "D1": "f1", "D2": "f2", "D3": "f3",
}
MESH = pl.DeviceIdType.MESH
RING = 8


def layer_norm(values, gains):
    average = jnp.mean(values, axis=-1, keepdims=True)
    centred = values - average
    variance = jnp.mean(centred * centred, axis=-1, keepdims=True)
    return centred * lax.rsqrt(variance + EPSILON) * gains


def rms_norm(values, gains):
    return values * lax.rsqrt(jnp.mean(values * values, axis=-1, keepdims=True) + EPSILON) * gains


def gelu(v):
    return 0.5 * v * (1.0 + lax.erf(v * math.sqrt(0.5)))


def slot_of(rel):
    if rel == 0:
        return 0
    if abs(rel) == 4:
        return 1
    return 2 * abs(rel) + (1 if rel > 0 else 0)


def vision_kernel(
    patch_ref, text_ref, vg_ref, mg_ref, dg_ref, slot_ref, doc_ref, wq_ref, wo_ref, w1_hbm, w2_hbm, wm_hbm,
    out_ref,
    win, relay, doc, wg, bias, total, xg, acc, w1, w2, wm, rs_out, rs_in, fsend, frx, psend, prx, mg, mine,
    local_sem, ws_sem, wr_sem, fs_sem, fr_sem, as_sem, ar_sem, rs_sem, rr_sem,
    ts_sem, tr_sem, ps_sem, pr_sem, gs_sem, gr_sem,
    ms_sem, mr_sem, ns_sem, nr_sem, zs_sem, zr_sem, ys_sem, yr_sem, y2s_sem, y2r_sem, os_sem, or_sem, ss_sem, sr_sem, hs_sem, hr_sem,
):
    r = lax.axis_index("req")
    t = lax.axis_index("tp")
    z = lax.rem(t, RING)
    xl = t // RING
    core = lax.rem(r, 2)
    xhi = lax.rem(r // 2, 2)
    inner = (r, (1 - xl) * RING + z)
    outer = (r + 2 - 4 * xhi, (1 - xl) * RING + z)
    sibling = (r + 1 - 2 * core, t)

    tp_size = 2 * RING
    after = (r, lax.rem(t + 1, tp_size))
    y_next, y_prev = (lax.rem(r + 4, 16), t), (lax.rem(r + 12, 16), t)

    def column(k):
        return (r, xl * RING + lax.rem(z + k + RING, RING))

    rows = patch_ref.shape[0]
    half = rows // 2

    def remote(src, dst, ssem, rsem, dev):
        return pltpu.make_async_remote_copy(
            src_ref=src, dst_ref=dst, send_sem=ssem, recv_sem=rsem, device_id=dev, device_id_type=MESH
        )

    pending = []

    def send(src, dst, ssem, rsem, dev):
        c = remote(src, dst, ssem, rsem, dev)
        c.start()
        pending.append(c)
        return c

    mg[...] = jnp.zeros_like(mg)
    barrier = pltpu.get_barrier_semaphore()
    peers = [(r, lax.rem(t + k, tp_size)) for k in range(1, tp_size)] + [outer, sibling, y_next, y_prev]
    for dev in peers:
        pl.semaphore_signal(barrier, inc=1, device_id=dev, device_id_type=MESH)

    loads = [
        pltpu.make_async_copy(w1_hbm, w1.at[0], local_sem.at[0]),
        pltpu.make_async_copy(w2_hbm, w2.at[0], local_sem.at[1]),
        pltpu.make_async_copy(wm_hbm, wm.at[xl], local_sem.at[2]),
    ]
    for c in loads:
        c.start()

    wide = patch_ref[...].astype(jnp.float32)
    xg[0] = layer_norm(wide, vg_ref[...].reshape(1, -1)).astype(jnp.bfloat16)
    pl.semaphore_wait(barrier, len(peers))

    ag = {}
    for d, s in ((0, 1), (1, -1)):
        ag[d, 0] = send(xg.at[0], xg.at[slot_of(-s)], as_sem.at[d, 0], ar_sem.at[d, 0], column(s))

    n1 = w1_hbm.shape[0] // 4
    n2 = w2_hbm.shape[0] // 4
    wx = []
    for i, dev in ((0, inner), (1, outer)):
        q = core * 2 + i
        a1 = pl.ds(pl.multiple_of(q * n1, 16), n1)
        a2 = pl.ds(pl.multiple_of(q * n2, 16), n2)
        wx.append((send(w1_hbm.at[a1], w1.at[1, a1], ws_sem.at[2 * i], wr_sem.at[2 * i], dev), w1.at[1, a1]))
        wx.append((send(w2_hbm.at[a2], w2.at[1, a2], ws_sem.at[2 * i + 1], wr_sem.at[2 * i + 1], dev), w2.at[1, a2]))
    quarter = wg.shape[1] // 4
    y = r // 4
    s_w = 1 - 2 * core
    ahead = column(s_w)

    def quarter_at(k):
        return pl.ds(pl.multiple_of(lax.rem(y + k, 4) * quarter, 16), quarter)

    def shard_at(k):
        return xl * RING + lax.rem(z - s_w * (k + 1) + RING, RING)

    mx = []

    def merge_weights():
        for i, dev in ((0, inner), (1, outer)):
            at = pl.ds(pl.multiple_of(core * 208 + 112 * i, 16), (112, 96)[i])
            mx.append((send(wm_hbm.at[at], wm.at[xl, at], ms_sem.at[i], mr_sem.at[i], dev), wm.at[1 - xl, at]))

    row = lax.broadcasted_iota(jnp.int32, (3 * quarter, 3 * HD), 0)
    col = lax.broadcasted_iota(jnp.int32, (3 * quarter, 3 * HD), 1)
    second = (row >= quarter).astype(jnp.int32)
    third = (row >= 2 * quarter).astype(jnp.int32)
    inside = row - quarter * (second + third)
    pick = (col == inside + HD * (1 + second - 2 * third)) & (inside < HD)
    pick = pick.astype(jnp.float32).astype(jnp.bfloat16)
    wg[t, :3 * quarter] = jnp.dot(pick, wq_ref[...], preferred_element_type=jnp.float32).astype(jnp.bfloat16)
    row = lax.broadcasted_iota(jnp.int32, (quarter, HD), 0)
    col = lax.broadcasted_iota(jnp.int32, (quarter, HD), 1)
    pick = (row == col).astype(jnp.float32).astype(jnp.bfloat16)
    wg[t, 3 * quarter:] = jnp.dot(pick, wo_ref[...], preferred_element_type=jnp.float32).astype(jnp.bfloat16)

    zc = []
    yc, y2c, xc, sc, hc = {}, {}, {}, [], []

    def from_column(k):
        if k < 0:
            zc.append(send(wg.at[t, quarter_at(0)], wg.at[t, quarter_at(0)], zs_sem.at[0], zr_sem.at[0], ahead))
            return
        piece = wg.at[shard_at(k), quarter_at(0)]
        zc[k].wait_recv()
        if k < 3:
            zc.append(send(piece, piece, zs_sem.at[k + 1], zr_sem.at[k + 1], ahead))
        yc[k] = (
            send(piece, piece, ys_sem.at[k, 0], yr_sem.at[k, 0], y_next),
            send(piece, piece, ys_sem.at[k, 1], yr_sem.at[k, 1], y_prev),
        )

    def from_y(k):
        for c in yc[k]:
            c.wait_recv()
        piece = wg.at[shard_at(k), quarter_at(3 if k % 2 == 0 else 1)]
        y2c[k] = send(piece, piece, y2s_sem.at[k], y2r_sem.at[k], y_next if k % 2 == 0 else y_prev)

    def both_halves(ref, i):
        n = wg.shape[1] // 2
        return ref.at[pl.ds(i * n, n)]

    def to_x(k):
        y2c[k].wait_recv()
        if k == 3:
            idx = xl * RING + lax.rem(z + 4 - 4 * core, RING)
        else:
            idx = shard_at(k)
        xc[k] = [
            send(both_halves(wg.at[idx], i), both_halves(wg.at[idx], i), os_sem.at[k, i], or_sem.at[k, i], dev)
            for i, dev in ((0, inner), (1, outer))
        ]
        if k < 3:
            sc.append(send(wg.at[idx], wg.at[idx], ss_sem.at[k], sr_sem.at[k], sibling))

    def from_x(k):
        if k == 3:
            idx = lax.rem(z + 4 - 4 * core, RING)
        else:
            idx = lax.rem(z - s_w * (k + 1) + RING, RING)
        idx = (1 - xl) * RING + idx
        for c in xc[k]:
            c.wait_recv()
        sc.append(send(wg.at[idx], wg.at[idx], ss_sem.at[3 + k], sr_sem.at[3 + k], sibling))

    cut = 128
    keep = slice(0, cut)
    rest = slice(cut, text_ref.shape[0])
    back = (r, lax.rem(t + tp_size - 1, tp_size))
    across = (r, lax.rem(xl * RING + lax.rem(z + 3, RING) + 4, tp_size))

    def window(k):
        if k > 0:
            for c in hc[-2:] if k < 5 else hc[-1:]:
                c.wait_recv()
        if k < 4:
            hc.append(send(win.at[k, keep], win.at[k + 1, keep], hs_sem.at[k], hr_sem.at[k], after))
        if k == 0:
            src, dst, dev = win.at[0, rest], relay, column(-3)
        elif k == 1:
            src, dst, dev = relay, win.at[4, rest], across
        elif k < 5:
            src, dst, dev = win.at[6 - k, rest], win.at[5 - k, rest], back
        if k < 5:
            hc.append(send(src, dst, hs_sem.at[4 + k], hr_sem.at[4 + k], dev))

    def serve(point):
        for name in PLAN.get(point, "").split():
            act = {"z": from_column, "y": from_y, "x": to_x, "f": from_x, "h": window}[name[0]]
            act(int(name[1:]))

    serve("S")

    def mlp(pair, which):
        x = xg[2 * pair:2 * pair + 2].reshape(2 * rows, xg.shape[2])
        h = gelu(jnp.dot(x, w1[which], preferred_element_type=jnp.float32)).astype(jnp.bfloat16)
        return jnp.dot(h, w2[which], preferred_element_type=jnp.float32).reshape(2, rows, w2.shape[2])

    for step in range(4):
        for d, s in ((0, 1), (1, -1)):
            rel = -s * (step + 1)
            ag[d, step].wait_recv()
            if step < 3:
                src, dst = xg.at[slot_of(rel)], xg.at[slot_of(rel - s)]
                if step == 2:
                    part = pl.ds(d * half, half)
                    src, dst = src.at[part], dst.at[part]
                ag[d, step + 1] = send(src, dst, as_sem.at[d, step + 1], ar_sem.at[d, step + 1], column(s))
        if step == 0:
            loads[0].wait()
            loads[1].wait()
        pair = (step + 1) % 4
        acc[2 * pair:2 * pair + 2] = mlp(pair, 0)
        if step == 0:
            win[0] = rms_norm(text_ref[...].astype(jnp.float32), dg_ref[...].reshape(1, -1)).astype(jnp.bfloat16)
        serve("A%d" % step)

    fwd = []
    for i, (c, ref) in enumerate(wx):
        c.wait_recv()
        fwd.append(send(ref, ref, fs_sem.at[i], fr_sem.at[i], sibling))
    merge_weights()
    for c in fwd:
        c.wait_recv()

    rs = {}
    for step in range(4):
        pair = (4 - step) % 4
        acc[2 * pair:2 * pair + 2] = acc[2 * pair:2 * pair + 2] + mlp(pair, 1)
        for d, s in ((0, 1), (1, -1)):
            block = acc.at[slot_of(s * (4 - step))]
            out = rs_out.at[d, step]
            if step == 0:
                part = pl.ds(d * half, half)
                out[part] = block[part].astype(jnp.bfloat16)
                rs[d, 0] = send(out.at[part], rs_in.at[d, 0, part], rs_sem.at[d, 0], rr_sem.at[d, 0], column(s))
                continue
            rs[d, step - 1].wait_recv()
            if step == 1:
                part = pl.ds(d * half, half)
                block[part] = block[part] + rs_in[d, 0, part].astype(jnp.float32)
                out[...] = block[...].astype(jnp.bfloat16)
            else:
                out[...] = (block[...] + rs_in[d, step - 1].astype(jnp.float32)).astype(jnp.bfloat16)
            rs[d, step] = send(out, rs_in.at[d, step], rs_sem.at[d, step], rr_sem.at[d, step], column(s))
        if step == 1:
            mf = []
            for i, (c, ref) in enumerate(mx):
                c.wait_recv()
                mf.append(send(ref, ref, ns_sem.at[i], nr_sem.at[i], sibling))
        serve("R%d" % step)
    rs[0, 3].wait_recv()
    rs[1, 3].wait_recv()
    summed = acc[0] + rs_in[0, 3].astype(jnp.float32) + rs_in[1, 3].astype(jnp.float32)
    nrm = layer_norm(patch_ref[...].astype(jnp.float32) + summed, mg_ref[...].reshape(1, -1)).astype(jnp.bfloat16)

    serve("L")
    mrows = rows // 4
    width = wm_hbm.shape[0]
    to_row = lax.broadcasted_iota(jnp.int32, (rows, rows), 0)
    from_row = lax.broadcasted_iota(jnp.int32, (rows, rows), 1)
    order = (4 * (to_row % mrows) + to_row // mrows == from_row).astype(jnp.bfloat16)
    nrm = jnp.dot(order, nrm, preferred_element_type=jnp.float32).astype(jnp.bfloat16)
    for p in range(4):
        line = nrm[p * mrows:(p + 1) * mrows]
        for c in range(4):
            j = 4 * p + c
            fsend[j % RING, j // RING] = line[:, c * width:(c + 1) * width]
    a2a = []
    for k in range(1, RING):
        dest = lax.rem(z + k, RING)
        a2a.append(send(fsend.at[dest], frx.at[RING - k], ts_sem.at[k], tr_sem.at[k], column(k)))
    frx[0] = fsend[z]
    serve("T")
    loads[2].wait()
    for c in mf:
        c.wait_recv()
    for c in a2a:
        c.wait_recv()

    part = jnp.dot(frx[:, 0].reshape(RING * mrows, width), wm[0], preferred_element_type=jnp.float32)
    part = part + jnp.dot(frx[:, 1].reshape(RING * mrows, width), wm[1], preferred_element_type=jnp.float32)
    psend[...] = part.reshape(psend.shape).astype(jnp.bfloat16)
    red = []
    for k in range(1, RING):
        red.append(send(psend.at[k], prx.at[RING - k], ps_sem.at[k], pr_sem.at[k], column(k)))
    serve("M")
    summed = part[:mrows]
    for c in red:
        c.wait_recv()
    for k in range(1, RING):
        summed = summed + prx[k].astype(jnp.float32)
    mine[...] = summed.astype(jnp.bfloat16)

    quad, lane4 = t // 4, lax.rem(t, 4)
    gat = []
    for i in range(2):
        for k in range(4):
            dest = lax.rem(quad + 2 + i, 4) * 4 + lax.rem(lane4 + k, 4)
            gat.append(send(mine, mg.at[t], gs_sem.at[4 * i + k], gr_sem.at[4 * i + k], (r, dest)))
    serve("G")

    seq = text_ref.shape[0]
    depth = wg.shape[1] // 2
    row = lax.broadcasted_iota(jnp.int32, (seq, seq), 0)
    col = lax.broadcasted_iota(jnp.int32, (seq, seq), 1)
    for k in range(tp_size):
        doc[k:k + 1] = doc_ref[:, k * seq:(k + 1) * seq].astype(jnp.float32)
    own = doc[pl.ds(t, 1), :]
    own = jnp.sum(jnp.where(row == col, own, 0.0), axis=1, keepdims=True)
    for k in range(5):
        theirs = doc[pl.ds(lax.rem(t - k + tp_size, tp_size), 1), :]
        kpos = (t - k) * seq + col
        allowed = (kpos >= 0) & (kpos <= t * seq + row) & (theirs == own)
        bias[:, k * seq:(k + 1) * seq] = jnp.where(allowed, 0.0, -1e30)
    serve("D0")
    for c in sc[:3]:
        c.wait_recv()
    for c in hc:
        c.wait_send()
    for c in gat:
        c.wait_recv()
    raw = mg[...].reshape(tp_size * mrows, mg.shape[2])
    image = rms_norm(raw.astype(jnp.float32), dg_ref[...].reshape(1, -1)).astype(jnp.bfloat16)
    for k in range(5):
        pos = (t - k) * seq + lax.broadcasted_iota(jnp.int32, (seq, 1), 0)
        onehot = (pos == slot_ref[...]).astype(jnp.float32)
        hit = jnp.max(onehot, axis=1, keepdims=True) > 0.0
        onehot = onehot.astype(jnp.bfloat16)
        placed = jnp.dot(onehot, image, preferred_element_type=jnp.float32)
        win[k] = jnp.where(hit, placed, win[k].astype(jnp.float32)).astype(jnp.bfloat16)
        if k == 0:
            placed = jnp.dot(onehot, raw, preferred_element_type=jnp.float32)
            total[...] = jnp.where(hit, placed, text_ref[...].astype(jnp.float32))

    lane = lax.broadcasted_iota(jnp.int32, (seq, depth), 1)
    split = depth // 2

    def decode(side, *pairs):
        heads = []
        for p in pairs:
            heads.append(side * RING + lax.rem(z + p, RING))
            heads.append(side * RING + lax.rem(z + RING - p + (4 if p == 0 else 0), RING))
        x = win[...].reshape(5 * seq, win.shape[2])
        first = win[0]
        kvs = [
            lax.dot_general(x, wg[h, :depth], NT, preferred_element_type=jnp.float32).astype(jnp.bfloat16)
            for h in heads
        ]
        qs = [lax.dot_general(first, wg[h, depth:], NT, preferred_element_type=jnp.float32) for h in heads]
        qs = [jnp.where(lane < split, q, 0.0).astype(jnp.bfloat16) for q in qs]
        scores = [
            lax.dot_general(q, kv, NT, preferred_element_type=jnp.float32) * (1.0 / math.sqrt(HD)) + bias[...]
            for q, kv in zip(qs, kvs)
        ]
        raised = [jnp.exp(s - jnp.max(s, axis=1, keepdims=True)) for s in scores]
        mass = [jnp.sum(e, axis=1, keepdims=True) for e in raised]
        mixed = [
            (jnp.dot(e.astype(jnp.bfloat16), kv, preferred_element_type=jnp.float32) / m)[:, split:]
            for e, kv, m in zip(raised, kvs, mass)
        ]
        outs = jnp.concatenate([wg[h, depth + split:] for h in heads], axis=0)
        mixed = jnp.concatenate(mixed, axis=1).astype(jnp.bfloat16)
        total[...] += jnp.dot(mixed, outs, preferred_element_type=jnp.float32)

    decode(xl, 0, 1)
    serve("D1")
    decode(xl, 2, 3)
    serve("D2")
    for c in sc[3:5]:
        c.wait_recv()
    decode(1 - xl, 1, 2)
    serve("D3")
    for c in sc[5:]:
        c.wait_recv()
    decode(1 - xl, 3, 0)
    out_ref[...] = total[...].astype(jnp.bfloat16)
    for c in pending:
        if not any(c is d for d in hc):
            c.wait_send()


NT = (((1,), (1,)), ((), ()))


def block(patches, text, vg, mgain, dgain, slots, docs, wq, wo, w1, w2, wm):
    rows, width = patches.shape
    seq = text.shape[0]
    hidden = w1.shape[1]
    mrows = rows // 4
    bf, f32 = jnp.bfloat16, jnp.float32
    dma = pltpu.SemaphoreType.DMA
    vmem = pl.BlockSpec(memory_space=pltpu.VMEM)
    hbm = pl.BlockSpec(memory_space=pl.ANY)
    return pl.pallas_call(
        vision_kernel,
        out_shape=jax.ShapeDtypeStruct((seq, width), bf),
        in_specs=[vmem] * 9 + [hbm] * 3,
        out_specs=vmem,
        scratch_shapes=[
            pltpu.VMEM((5, seq, width), bf),
            pltpu.VMEM((seq - 128, width), bf),
            pltpu.VMEM((16, seq), f32),
            pltpu.VMEM((16, 4 * 112, width), bf),
            pltpu.VMEM((seq, 5 * seq), f32),
            pltpu.VMEM((seq, width), f32),
            pltpu.VMEM((8, rows, width), bf),
            pltpu.VMEM((8, rows, width), f32),
            pltpu.VMEM((2, width, hidden), bf),
            pltpu.VMEM((2, hidden, width), bf),
            pltpu.VMEM((2, wm.shape[0], width), bf),
            pltpu.VMEM((2, 4, rows, width), bf),
            pltpu.VMEM((2, 4, rows, width), bf),
            pltpu.VMEM((8, 2, mrows, wm.shape[0]), bf),
            pltpu.VMEM((8, 2, mrows, wm.shape[0]), bf),
            pltpu.VMEM((8, mrows, width), bf),
            pltpu.VMEM((8, mrows, width), bf),
            pltpu.VMEM((16, mrows, width), bf),
            pltpu.VMEM((mrows, width), bf),
            dma((4,)), dma((4,)), dma((4,)), dma((4,)), dma((4,)),
            dma((2, 4)), dma((2, 4)), dma((2, 4)), dma((2, 4)),
            dma((8,)), dma((8,)), dma((8,)), dma((8,)), dma((8,)), dma((8,)),
            dma((2,)), dma((2,)), dma((2,)), dma((2,)),
            dma((4,)), dma((4,)), dma((4, 2)), dma((4, 2)), dma((4,)), dma((4,)),
            dma((4, 2)), dma((4, 2)), dma((7,)), dma((7,)), dma((9,)), dma((9,)),
        ],
        compiler_params=pltpu.CompilerParams(
            collective_id=0, has_side_effects=True, vmem_limit_bytes=62 * 2**20
        ),
        name="block",
    )(patches, text, vg, mgain, dgain, slots, docs, wq, wo, w1, w2, wm)


def shards(
    patches, vis_gain, w_fc1, w_fc2, merge_gain, w_merge, slots, text, docs, dec_gain, w_qkv, w_out
):
    text_rows = text[0]
    out = block(
        patches[0], text_rows, vis_gain, merge_gain, dec_gain, slots, docs, w_qkv.T, w_out,
        w_fc1, w_fc2, w_merge,
    )
    return out[None]


def solution(mesh):
    placed = (
        P("req", "tp", None),
        P(),
        P(None, "tp"),
        P("tp", None),
        P(),
        P("tp", None),
        P("req", None),
        P("req", "tp", None),
        P("req", None),
        P(),
        P(None, "tp"),
        P("tp", None),
    )
    return jax.shard_map(
        shards, mesh=mesh, in_specs=placed, out_specs=P("req", "tp", None), check_vma=False
    )
```

```python
import functools
import math

import jax
import jax.numpy as jnp
from jax import lax
from jax.experimental import pallas as pl
from jax.experimental.pallas import tpu as pltpu
from jax.sharding import PartitionSpec as P

HD = 104
EPSILON = 1e-06
PLAN = {
    "A1": "z-1", "A2": "z0", "A3": "z1 h0", "R0": "z2 y0", "R1": "z3", "R2": "y1 x0", "R3": "y2 h1", "L": "x1",
    "T": "y3 h2", "M": "x2 h3", "G": "x3 f0 h4", "D0": "h5", "D1": "f1", "D2": "f2", "D3": "f3",
}
MESH = pl.DeviceIdType.MESH
RING = 8


def layer_norm(values, gains):
    average = jnp.mean(values, axis=-1, keepdims=True)
    centred = values - average
    variance = jnp.mean(centred * centred, axis=-1, keepdims=True)
    return centred * lax.rsqrt(variance + EPSILON) * gains


def rms_norm(values, gains):
    return values * lax.rsqrt(jnp.mean(values * values, axis=-1, keepdims=True) + EPSILON) * gains


def gelu(v):
    return 0.5 * v * (1.0 + lax.erf(v * math.sqrt(0.5)))


def slot_of(rel):
    if rel == 0:
        return 0
    if abs(rel) == 4:
        return 1
    return 2 * abs(rel) + (1 if rel > 0 else 0)


def vision_kernel(
    patch_ref, text_ref, vg_ref, mg_ref, dg_ref, slot_ref, doc_ref, wq_ref, wo_ref, w1_hbm, w2_hbm, wm_hbm,
    out_ref,
    win, relay, doc, wg, bias, total, xg, acc, w1, w2, wm, rs_out, rs_in, fsend, frx, psend, prx, mg, mine,
    local_sem, ws_sem, wr_sem, fs_sem, fr_sem, as_sem, ar_sem, rs_sem, rr_sem,
    ts_sem, tr_sem, ps_sem, pr_sem, gs_sem, gr_sem,
    ms_sem, mr_sem, ns_sem, nr_sem, zs_sem, zr_sem, ys_sem, yr_sem, y2s_sem, y2r_sem, os_sem, or_sem, ss_sem, sr_sem, hs_sem, hr_sem,
):
    r = lax.axis_index("req")
    t = lax.axis_index("tp")
    z = lax.rem(t, RING)
    xl = t // RING
    core = lax.rem(r, 2)
    xhi = lax.rem(r // 2, 2)
    inner = (r, (1 - xl) * RING + z)
    outer = (r + 2 - 4 * xhi, (1 - xl) * RING + z)
    sibling = (r + 1 - 2 * core, t)

    tp_size = 2 * RING
    after = (r, lax.rem(t + 1, tp_size))
    y_next, y_prev = (lax.rem(r + 4, 16), t), (lax.rem(r + 12, 16), t)

    def column(k):
        return (r, xl * RING + lax.rem(z + k + RING, RING))

    rows = patch_ref.shape[0]
    half = rows // 2

    def remote(src, dst, ssem, rsem, dev):
        return pltpu.make_async_remote_copy(
            src_ref=src, dst_ref=dst, send_sem=ssem, recv_sem=rsem, device_id=dev, device_id_type=MESH
        )

    pending = []

    def send(src, dst, ssem, rsem, dev):
        c = remote(src, dst, ssem, rsem, dev)
        c.start()
        pending.append(c)
        return c

    mg[...] = jnp.zeros_like(mg)
    barrier = pltpu.get_barrier_semaphore()
    peers = [(r, lax.rem(t + k, tp_size)) for k in range(1, tp_size)] + [outer, sibling, y_next, y_prev]
    for dev in peers:
        pl.semaphore_signal(barrier, inc=1, device_id=dev, device_id_type=MESH)

    loads = [
        pltpu.make_async_copy(w1_hbm, w1.at[0], local_sem.at[0]),
        pltpu.make_async_copy(w2_hbm, w2.at[0], local_sem.at[1]),
        pltpu.make_async_copy(wm_hbm, wm.at[xl], local_sem.at[2]),
    ]
    for c in loads:
        c.start()

    wide = patch_ref[...].astype(jnp.float32)
    xg[0] = layer_norm(wide, vg_ref[...].reshape(1, -1)).astype(jnp.bfloat16)
    pl.semaphore_wait(barrier, len(peers))

    ag = {}
    for d, s in ((0, 1), (1, -1)):
        ag[d, 0] = send(xg.at[0], xg.at[slot_of(-s)], as_sem.at[d, 0], ar_sem.at[d, 0], column(s))

    n1 = w1_hbm.shape[0] // 4
    n2 = w2_hbm.shape[0] // 4
    wx = []
    for i, dev in ((0, inner), (1, outer)):
        q = core * 2 + i
        a1 = pl.ds(pl.multiple_of(q * n1, 16), n1)
        a2 = pl.ds(pl.multiple_of(q * n2, 16), n2)
        wx.append((send(w1_hbm.at[a1], w1.at[1, a1], ws_sem.at[2 * i], wr_sem.at[2 * i], dev), w1.at[1, a1]))
        wx.append((send(w2_hbm.at[a2], w2.at[1, a2], ws_sem.at[2 * i + 1], wr_sem.at[2 * i + 1], dev), w2.at[1, a2]))
    quarter = wg.shape[1] // 4
    y = r // 4
    s_w = 1 - 2 * core
    ahead = column(s_w)

    def quarter_at(k):
        return pl.ds(pl.multiple_of(lax.rem(y + k, 4) * quarter, 16), quarter)

    def shard_at(k):
        return xl * RING + lax.rem(z - s_w * (k + 1) + RING, RING)

    mx = []

    def merge_weights():
        for i, dev in ((0, inner), (1, outer)):
            at = pl.ds(pl.multiple_of(core * 208 + 112 * i, 16), (112, 96)[i])
            mx.append((send(wm_hbm.at[at], wm.at[xl, at], ms_sem.at[i], mr_sem.at[i], dev), wm.at[1 - xl, at]))

    row = lax.broadcasted_iota(jnp.int32, (3 * quarter, 3 * HD), 0)
    col = lax.broadcasted_iota(jnp.int32, (3 * quarter, 3 * HD), 1)
    second = (row >= quarter).astype(jnp.int32)
    third = (row >= 2 * quarter).astype(jnp.int32)
    inside = row - quarter * (second + third)
    pick = (col == inside + HD * (1 + second - 2 * third)) & (inside < HD)
    pick = pick.astype(jnp.float32).astype(jnp.bfloat16)
    wg[t, :3 * quarter] = jnp.dot(pick, wq_ref[...], preferred_element_type=jnp.float32).astype(jnp.bfloat16)
    row = lax.broadcasted_iota(jnp.int32, (quarter, HD), 0)
    col = lax.broadcasted_iota(jnp.int32, (quarter, HD), 1)
    pick = (row == col).astype(jnp.float32).astype(jnp.bfloat16)
    wg[t, 3 * quarter:] = jnp.dot(pick, wo_ref[...], preferred_element_type=jnp.float32).astype(jnp.bfloat16)

    zc = []
    yc, y2c, xc, sc, hc = {}, {}, {}, [], []

    def from_column(k):
        if k < 0:
            zc.append(send(wg.at[t, quarter_at(0)], wg.at[t, quarter_at(0)], zs_sem.at[0], zr_sem.at[0], ahead))
            return
        piece = wg.at[shard_at(k), quarter_at(0)]
        zc[k].wait_recv()
        if k < 3:
            zc.append(send(piece, piece, zs_sem.at[k + 1], zr_sem.at[k + 1], ahead))
        yc[k] = (
            send(piece, piece, ys_sem.at[k, 0], yr_sem.at[k, 0], y_next),
            send(piece, piece, ys_sem.at[k, 1], yr_sem.at[k, 1], y_prev),
        )

    def from_y(k):
        for c in yc[k]:
            c.wait_recv()
        piece = wg.at[shard_at(k), quarter_at(3 if k % 2 == 0 else 1)]
        y2c[k] = send(piece, piece, y2s_sem.at[k], y2r_sem.at[k], y_next if k % 2 == 0 else y_prev)

    def both_halves(ref, i):
        n = wg.shape[1] // 2
        return ref.at[pl.ds(i * n, n)]

    def to_x(k):
        y2c[k].wait_recv()
        if k == 3:
            idx = xl * RING + lax.rem(z + 4 - 4 * core, RING)
        else:
            idx = shard_at(k)
        xc[k] = [
            send(both_halves(wg.at[idx], i), both_halves(wg.at[idx], i), os_sem.at[k, i], or_sem.at[k, i], dev)
            for i, dev in ((0, inner), (1, outer))
        ]
        if k < 3:
            sc.append(send(wg.at[idx], wg.at[idx], ss_sem.at[k], sr_sem.at[k], sibling))

    def from_x(k):
        if k == 3:
            idx = lax.rem(z + 4 - 4 * core, RING)
        else:
            idx = lax.rem(z - s_w * (k + 1) + RING, RING)
        idx = (1 - xl) * RING + idx
        for c in xc[k]:
            c.wait_recv()
        sc.append(send(wg.at[idx], wg.at[idx], ss_sem.at[3 + k], sr_sem.at[3 + k], sibling))

    cut = 128
    keep = slice(0, cut)
    rest = slice(cut, text_ref.shape[0])
    back = (r, lax.rem(t + tp_size - 1, tp_size))
    across = (r, lax.rem(xl * RING + lax.rem(z + 3, RING) + 4, tp_size))

    def window(k):
        if k > 0:
            for c in hc[-2:] if k < 5 else hc[-1:]:
                c.wait_recv()
        if k < 4:
            hc.append(send(win.at[k, keep], win.at[k + 1, keep], hs_sem.at[k], hr_sem.at[k], after))
        if k == 0:
            src, dst, dev = win.at[0, rest], relay, column(-3)
        elif k == 1:
            src, dst, dev = relay, win.at[4, rest], across
        elif k < 5:
            src, dst, dev = win.at[6 - k, rest], win.at[5 - k, rest], back
        if k < 5:
            hc.append(send(src, dst, hs_sem.at[4 + k], hr_sem.at[4 + k], dev))

    def serve(point):
        for name in PLAN.get(point, "").split():
            act = {"z": from_column, "y": from_y, "x": to_x, "f": from_x, "h": window}[name[0]]
            act(int(name[1:]))

    serve("S")

    def mlp(pair, which):
        x = xg[2 * pair:2 * pair + 2].reshape(2 * rows, xg.shape[2])
        h = gelu(jnp.dot(x, w1[which], preferred_element_type=jnp.float32)).astype(jnp.bfloat16)
        return jnp.dot(h, w2[which], preferred_element_type=jnp.float32).reshape(2, rows, w2.shape[2])

    for step in range(4):
        for d, s in ((0, 1), (1, -1)):
            rel = -s * (step + 1)
            ag[d, step].wait_recv()
            if step < 3:
                src, dst = xg.at[slot_of(rel)], xg.at[slot_of(rel - s)]
                if step == 2:
                    part = pl.ds(d * half, half)
                    src, dst = src.at[part], dst.at[part]
                ag[d, step + 1] = send(src, dst, as_sem.at[d, step + 1], ar_sem.at[d, step + 1], column(s))
        if step == 0:
            loads[0].wait()
            loads[1].wait()
        pair = (step + 1) % 4
        acc[2 * pair:2 * pair + 2] = mlp(pair, 0)
        if step == 0:
            win[0] = rms_norm(text_ref[...].astype(jnp.float32), dg_ref[...].reshape(1, -1)).astype(jnp.bfloat16)
        serve("A%d" % step)

    fwd = []
    for i, (c, ref) in enumerate(wx):
        c.wait_recv()
        fwd.append(send(ref, ref, fs_sem.at[i], fr_sem.at[i], sibling))
    merge_weights()
    for c in fwd:
        c.wait_recv()

    rs = {}
    for step in range(4):
        pair = (4 - step) % 4
        acc[2 * pair:2 * pair + 2] = acc[2 * pair:2 * pair + 2] + mlp(pair, 1)
        for d, s in ((0, 1), (1, -1)):
            block = acc.at[slot_of(s * (4 - step))]
            out = rs_out.at[d, step]
            if step == 0:
                part = pl.ds(d * half, half)
                out[part] = block[part].astype(jnp.bfloat16)
                rs[d, 0] = send(out.at[part], rs_in.at[d, 0, part], rs_sem.at[d, 0], rr_sem.at[d, 0], column(s))
                continue
            rs[d, step - 1].wait_recv()
            if step == 1:
                part = pl.ds(d * half, half)
                block[part] = block[part] + rs_in[d, 0, part].astype(jnp.float32)
                out[...] = block[...].astype(jnp.bfloat16)
            else:
                out[...] = (block[...] + rs_in[d, step - 1].astype(jnp.float32)).astype(jnp.bfloat16)
            rs[d, step] = send(out, rs_in.at[d, step], rs_sem.at[d, step], rr_sem.at[d, step], column(s))
        if step == 1:
            mf = []
            for i, (c, ref) in enumerate(mx):
                c.wait_recv()
                mf.append(send(ref, ref, ns_sem.at[i], nr_sem.at[i], sibling))
        serve("R%d" % step)
    rs[0, 3].wait_recv()
    rs[1, 3].wait_recv()
    summed = acc[0] + rs_in[0, 3].astype(jnp.float32) + rs_in[1, 3].astype(jnp.float32)
    nrm = layer_norm(patch_ref[...].astype(jnp.float32) + summed, mg_ref[...].reshape(1, -1)).astype(jnp.bfloat16)

    serve("L")
    mrows = rows // 4
    width = wm_hbm.shape[0]
    to_row = lax.broadcasted_iota(jnp.int32, (rows, rows), 0)
    from_row = lax.broadcasted_iota(jnp.int32, (rows, rows), 1)
    order = (4 * (to_row % mrows) + to_row // mrows == from_row).astype(jnp.bfloat16)
    nrm = jnp.dot(order, nrm, preferred_element_type=jnp.float32).astype(jnp.bfloat16)
    for p in range(4):
        line = nrm[p * mrows:(p + 1) * mrows]
        for c in range(4):
            j = 4 * p + c
            fsend[j % RING, j // RING] = line[:, c * width:(c + 1) * width]
    a2a = []
    for k in range(1, RING):
        dest = lax.rem(z + k, RING)
        a2a.append(send(fsend.at[dest], frx.at[RING - k], ts_sem.at[k], tr_sem.at[k], column(k)))
    frx[0] = fsend[z]
    serve("T")
    loads[2].wait()
    for c in mf:
        c.wait_recv()
    for c in a2a:
        c.wait_recv()

    part = jnp.dot(frx[:, 0].reshape(RING * mrows, width), wm[0], preferred_element_type=jnp.float32)
    part = part + jnp.dot(frx[:, 1].reshape(RING * mrows, width), wm[1], preferred_element_type=jnp.float32)
    psend[...] = part.reshape(psend.shape).astype(jnp.bfloat16)
    red = []
    for k in range(1, RING):
        red.append(send(psend.at[k], prx.at[RING - k], ps_sem.at[k], pr_sem.at[k], column(k)))
    serve("M")
    summed = part[:mrows]
    for c in red:
        c.wait_recv()
    for k in range(1, RING):
        summed = summed + prx[k].astype(jnp.float32)
    mine[...] = summed.astype(jnp.bfloat16)

    quad, lane4 = t // 4, lax.rem(t, 4)
    gat = []
    for i in range(2):
        for k in range(4):
            dest = lax.rem(quad + 2 + i, 4) * 4 + lax.rem(lane4 + k, 4)
            gat.append(send(mine, mg.at[t], gs_sem.at[4 * i + k], gr_sem.at[4 * i + k], (r, dest)))
    serve("G")

    seq = text_ref.shape[0]
    depth = wg.shape[1] // 2
    row = lax.broadcasted_iota(jnp.int32, (seq, seq), 0)
    col = lax.broadcasted_iota(jnp.int32, (seq, seq), 1)
    for k in range(tp_size):
        doc[k:k + 1] = doc_ref[:, k * seq:(k + 1) * seq].astype(jnp.float32)
    own = doc[pl.ds(t, 1), :]
    own = jnp.sum(jnp.where(row == col, own, 0.0), axis=1, keepdims=True)
    for k in range(5):
        theirs = doc[pl.ds(lax.rem(t - k + tp_size, tp_size), 1), :]
        kpos = (t - k) * seq + col
        allowed = (kpos >= 0) & (kpos <= t * seq + row) & (theirs == own)
        bias[:, k * seq:(k + 1) * seq] = jnp.where(allowed, 0.0, -1e30)
    serve("D0")
    for c in sc[:3]:
        c.wait_recv()
    for c in hc:
        c.wait_send()
    for c in gat:
        c.wait_recv()
    raw = mg[...].reshape(tp_size * mrows, mg.shape[2])
    image = rms_norm(raw.astype(jnp.float32), dg_ref[...].reshape(1, -1)).astype(jnp.bfloat16)
    for k in range(5):
        pos = (t - k) * seq + lax.broadcasted_iota(jnp.int32, (seq, 1), 0)
        onehot = (pos == slot_ref[...]).astype(jnp.float32)
        hit = jnp.max(onehot, axis=1, keepdims=True) > 0.0
        onehot = onehot.astype(jnp.bfloat16)
        placed = jnp.dot(onehot, image, preferred_element_type=jnp.float32)
        win[k] = jnp.where(hit, placed, win[k].astype(jnp.float32)).astype(jnp.bfloat16)
        if k == 0:
            placed = jnp.dot(onehot, raw, preferred_element_type=jnp.float32)
            total[...] = jnp.where(hit, placed, text_ref[...].astype(jnp.float32))

    lane = lax.broadcasted_iota(jnp.int32, (seq, depth), 1)
    split = depth // 2

    def decode(side, *pairs):
        heads = []
        for p in pairs:
            heads.append(side * RING + lax.rem(z + p, RING))
            heads.append(side * RING + lax.rem(z + RING - p + (4 if p == 0 else 0), RING))
        x = win[...].reshape(5 * seq, win.shape[2])
        first = win[0]
        kvs = [
            lax.dot_general(x, wg[h, :depth], NT, preferred_element_type=jnp.float32).astype(jnp.bfloat16)
            for h in heads
        ]
        qs = [lax.dot_general(first, wg[h, depth:], NT, preferred_element_type=jnp.float32) for h in heads]
        qs = [jnp.where(lane < split, q, 0.0).astype(jnp.bfloat16) for q in qs]
        scores = [
            lax.dot_general(q, kv, NT, preferred_element_type=jnp.float32) * (1.0 / math.sqrt(HD)) + bias[...]
            for q, kv in zip(qs, kvs)
        ]
        raised = [jnp.exp(s - jnp.max(s, axis=1, keepdims=True)) for s in scores]
        mass = [jnp.sum(e, axis=1, keepdims=True) for e in raised]
        mixed = [
            (jnp.dot(e.astype(jnp.bfloat16), kv, preferred_element_type=jnp.float32) / m)[:, split:]
            for e, kv, m in zip(raised, kvs, mass)
        ]
        outs = jnp.concatenate([wg[h, depth + split:] for h in heads], axis=0)
        mixed = jnp.concatenate(mixed, axis=1).astype(jnp.bfloat16)
        total[...] += jnp.dot(mixed, outs, preferred_element_type=jnp.float32)

    decode(xl, 0, 1)
    serve("D1")
    decode(xl, 2, 3)
    serve("D2")
    for c in sc[3:5]:
        c.wait_recv()
    decode(1 - xl, 1, 2)
    serve("D3")
    for c in sc[5:]:
        c.wait_recv()
    decode(1 - xl, 3, 0)
    out_ref[...] = total[...].astype(jnp.bfloat16)
    for c in pending:
        if not any(c is d for d in hc):
            c.wait_send()


NT = (((1,), (1,)), ((), ()))


def block(patches, text, vg, mgain, dgain, slots, docs, wq, wo, w1, w2, wm):
    rows, width = patches.shape
    seq = text.shape[0]
    hidden = w1.shape[1]
    mrows = rows // 4
    bf, f32 = jnp.bfloat16, jnp.float32
    dma = pltpu.SemaphoreType.DMA
    vmem = pl.BlockSpec(memory_space=pltpu.VMEM)
    hbm = pl.BlockSpec(memory_space=pl.ANY)
    return pl.pallas_call(
        vision_kernel,
        out_shape=jax.ShapeDtypeStruct((seq, width), bf),
        in_specs=[vmem] * 9 + [hbm] * 3,
        out_specs=vmem,
        scratch_shapes=[
            pltpu.VMEM((5, seq, width), bf),
            pltpu.VMEM((seq - 128, width), bf),
            pltpu.VMEM((16, seq), f32),
            pltpu.VMEM((16, 4 * 112, width), bf),
            pltpu.VMEM((seq, 5 * seq), f32),
            pltpu.VMEM((seq, width), f32),
            pltpu.VMEM((8, rows, width), bf),
            pltpu.VMEM((8, rows, width), f32),
            pltpu.VMEM((2, width, hidden), bf),
            pltpu.VMEM((2, hidden, width), bf),
            pltpu.VMEM((2, wm.shape[0], width), bf),
            pltpu.VMEM((2, 4, rows, width), bf),
            pltpu.VMEM((2, 4, rows, width), bf),
            pltpu.VMEM((8, 2, mrows, wm.shape[0]), bf),
            pltpu.VMEM((8, 2, mrows, wm.shape[0]), bf),
            pltpu.VMEM((8, mrows, width), bf),
            pltpu.VMEM((8, mrows, width), bf),
            pltpu.VMEM((16, mrows, width), bf),
            pltpu.VMEM((mrows, width), bf),
            dma((4,)), dma((4,)), dma((4,)), dma((4,)), dma((4,)),
            dma((2, 4)), dma((2, 4)), dma((2, 4)), dma((2, 4)),
            dma((8,)), dma((8,)), dma((8,)), dma((8,)), dma((8,)), dma((8,)),
            dma((2,)), dma((2,)), dma((2,)), dma((2,)),
            dma((4,)), dma((4,)), dma((4, 2)), dma((4, 2)), dma((4,)), dma((4,)),
            dma((4, 2)), dma((4, 2)), dma((7,)), dma((7,)), dma((9,)), dma((9,)),
        ],
        compiler_params=pltpu.CompilerParams(
            collective_id=0, has_side_effects=True, vmem_limit_bytes=62 * 2**20
        ),
        name="block",
    )(patches, text, vg, mgain, dgain, slots, docs, wq, wo, w1, w2, wm)


def shards(
    patches, vis_gain, w_fc1, w_fc2, merge_gain, w_merge, slots, text, docs, dec_gain, w_qkv, w_out
):
    text_rows = text[0]
    out = block(
        patches[0], text_rows, vis_gain, merge_gain, dec_gain, slots, docs, w_qkv.T, w_out,
        w_fc1, w_fc2, w_merge,
    )
    return out[None]


def solution(mesh):
    placed = (
        P("req", "tp", None),
        P(),
        P(None, "tp"),
        P("tp", None),
        P(),
        P("tp", None),
        P("req", None),
        P("req", "tp", None),
        P("req", None),
        P(),
        P(None, "tp"),
        P("tp", None),
    )
    return jax.shard_map(
        shards, mesh=mesh, in_specs=placed, out_specs=P("req", "tp", None), check_vma=False
    )
```

```python
import functools
import math

import jax
import jax.numpy as jnp
from jax import lax
from jax.experimental import pallas as pl
from jax.experimental.pallas import tpu as pltpu
from jax.sharding import PartitionSpec as P

HD = 104
EPSILON = 1e-06
PLAN = {
    "A0": "h0", "A3": "h1 z-1", "R0": "z0", "R1": "z1 h2", "R2": "z2 y0", "R3": "h3 z3", "L": "y1 x0",
    "T": "h4 y2 x1", "M": "h5 y3 x2", "G": "x3", "D0": "f0", "D1": "f1", "D2": "f2", "D3": "f3",
}
MESH = pl.DeviceIdType.MESH
RING = 8


def layer_norm(values, gains):
    average = jnp.mean(values, axis=-1, keepdims=True)
    centred = values - average
    variance = jnp.mean(centred * centred, axis=-1, keepdims=True)
    return centred * lax.rsqrt(variance + EPSILON) * gains


def rms_norm(values, gains):
    return values * lax.rsqrt(jnp.mean(values * values, axis=-1, keepdims=True) + EPSILON) * gains


def gelu(v):
    return 0.5 * v * (1.0 + lax.erf(v * math.sqrt(0.5)))


def slot_of(rel):
    if rel == 0:
        return 0
    if abs(rel) == 4:
        return 1
    return 2 * abs(rel) + (1 if rel > 0 else 0)


def vision_kernel(
    patch_ref, text_ref, vg_ref, mg_ref, dg_ref, slot_ref, doc_ref, wq_ref, wo_ref, w1_hbm, w2_hbm, wm_hbm,
    out_ref,
    win, relay, doc, wg, bias, total, xg, acc, w1, w2, wm, rs_out, rs_in, fsend, frx, psend, prx, mg, mine,
    local_sem, ws_sem, wr_sem, fs_sem, fr_sem, as_sem, ar_sem, rs_sem, rr_sem,
    ts_sem, tr_sem, ps_sem, pr_sem, gs_sem, gr_sem,
    ms_sem, mr_sem, ns_sem, nr_sem, zs_sem, zr_sem, ys_sem, yr_sem, y2s_sem, y2r_sem, os_sem, or_sem, ss_sem, sr_sem, hs_sem, hr_sem,
):
    r = lax.axis_index("req")
    t = lax.axis_index("tp")
    z = lax.rem(t, RING)
    xl = t // RING
    core = lax.rem(r, 2)
    xhi = lax.rem(r // 2, 2)
    inner = (r, (1 - xl) * RING + z)
    outer = (r + 2 - 4 * xhi, (1 - xl) * RING + z)
    sibling = (r + 1 - 2 * core, t)

    tp_size = 2 * RING
    after = (r, lax.rem(t + 1, tp_size))
    y_next, y_prev = (lax.rem(r + 4, 16), t), (lax.rem(r + 12, 16), t)

    def column(k):
        return (r, xl * RING + lax.rem(z + k + RING, RING))

    rows = patch_ref.shape[0]
    half = rows // 2

    def remote(src, dst, ssem, rsem, dev):
        return pltpu.make_async_remote_copy(
            src_ref=src, dst_ref=dst, send_sem=ssem, recv_sem=rsem, device_id=dev, device_id_type=MESH
        )

    pending = []

    def send(src, dst, ssem, rsem, dev):
        c = remote(src, dst, ssem, rsem, dev)
        c.start()
        pending.append(c)
        return c

    mg[...] = jnp.zeros_like(mg)
    barrier = pltpu.get_barrier_semaphore()
    peers = [(r, lax.rem(t + k, tp_size)) for k in range(1, tp_size)] + [outer, sibling, y_next, y_prev]
    for dev in peers:
        pl.semaphore_signal(barrier, inc=1, device_id=dev, device_id_type=MESH)

    loads = [
        pltpu.make_async_copy(w1_hbm, w1.at[0], local_sem.at[0]),
        pltpu.make_async_copy(w2_hbm, w2.at[0], local_sem.at[1]),
        pltpu.make_async_copy(wm_hbm, wm.at[xl], local_sem.at[2]),
    ]
    for c in loads:
        c.start()

    wide = patch_ref[...].astype(jnp.float32)
    xg[0] = layer_norm(wide, vg_ref[...].reshape(1, -1)).astype(jnp.bfloat16)
    pl.semaphore_wait(barrier, len(peers))

    ag = {}
    for d, s in ((0, 1), (1, -1)):
        ag[d, 0] = send(xg.at[0], xg.at[slot_of(-s)], as_sem.at[d, 0], ar_sem.at[d, 0], column(s))

    n1 = w1_hbm.shape[0] // 4
    n2 = w2_hbm.shape[0] // 4
    wx = []
    for i, dev in ((0, inner), (1, outer)):
        q = core * 2 + i
        a1 = pl.ds(pl.multiple_of(q * n1, 16), n1)
        a2 = pl.ds(pl.multiple_of(q * n2, 16), n2)
        wx.append((send(w1_hbm.at[a1], w1.at[1, a1], ws_sem.at[2 * i], wr_sem.at[2 * i], dev), w1.at[1, a1]))
        wx.append((send(w2_hbm.at[a2], w2.at[1, a2], ws_sem.at[2 * i + 1], wr_sem.at[2 * i + 1], dev), w2.at[1, a2]))
    quarter = wg.shape[1] // 4
    y = r // 4
    s_w = 1 - 2 * core
    ahead = column(s_w)

    def quarter_at(k):
        return pl.ds(pl.multiple_of(lax.rem(y + k, 4) * quarter, 16), quarter)

    def shard_at(k):
        return xl * RING + lax.rem(z - s_w * (k + 1) + RING, RING)

    mx = []

    def merge_weights():
        for i, dev in ((0, inner), (1, outer)):
            at = pl.ds(pl.multiple_of(core * 208 + 112 * i, 16), (112, 96)[i])
            mx.append((send(wm_hbm.at[at], wm.at[xl, at], ms_sem.at[i], mr_sem.at[i], dev), wm.at[1 - xl, at]))

    row = lax.broadcasted_iota(jnp.int32, (3 * quarter, 3 * HD), 0)
    col = lax.broadcasted_iota(jnp.int32, (3 * quarter, 3 * HD), 1)
    second = (row >= quarter).astype(jnp.int32)
    third = (row >= 2 * quarter).astype(jnp.int32)
    inside = row - quarter * (second + third)
    pick = (col == inside + HD * (1 + second - 2 * third)) & (inside < HD)
    pick = pick.astype(jnp.float32).astype(jnp.bfloat16)
    wg[t, :3 * quarter] = jnp.dot(pick, wq_ref[...], preferred_element_type=jnp.float32).astype(jnp.bfloat16)
    row = lax.broadcasted_iota(jnp.int32, (quarter, HD), 0)
    col = lax.broadcasted_iota(jnp.int32, (quarter, HD), 1)
    pick = (row == col).astype(jnp.float32).astype(jnp.bfloat16)
    wg[t, 3 * quarter:] = jnp.dot(pick, wo_ref[...], preferred_element_type=jnp.float32).astype(jnp.bfloat16)

    zc = []
    yc, y2c, xc, sc, hc = {}, {}, {}, [], []

    def from_column(k):
        if k < 0:
            zc.append(send(wg.at[t, quarter_at(0)], wg.at[t, quarter_at(0)], zs_sem.at[0], zr_sem.at[0], ahead))
            return
        piece = wg.at[shard_at(k), quarter_at(0)]
        zc[k].wait_recv()
        if k < 3:
            zc.append(send(piece, piece, zs_sem.at[k + 1], zr_sem.at[k + 1], ahead))
        yc[k] = (
            send(piece, piece, ys_sem.at[k, 0], yr_sem.at[k, 0], y_next),
            send(piece, piece, ys_sem.at[k, 1], yr_sem.at[k, 1], y_prev),
        )

    def from_y(k):
        for c in yc[k]:
            c.wait_recv()
        piece = wg.at[shard_at(k), quarter_at(3 if k % 2 == 0 else 1)]
        y2c[k] = send(piece, piece, y2s_sem.at[k], y2r_sem.at[k], y_next if k % 2 == 0 else y_prev)

    def both_halves(ref, i):
        n = wg.shape[1] // 2
        return ref.at[pl.ds(i * n, n)]

    def to_x(k):
        y2c[k].wait_recv()
        if k == 3:
            idx = xl * RING + lax.rem(z + 4 - 4 * core, RING)
        else:
            idx = shard_at(k)
        xc[k] = [
            send(both_halves(wg.at[idx], i), both_halves(wg.at[idx], i), os_sem.at[k, i], or_sem.at[k, i], dev)
            for i, dev in ((0, inner), (1, outer))
        ]
        if k < 3:
            sc.append(send(wg.at[idx], wg.at[idx], ss_sem.at[k], sr_sem.at[k], sibling))

    def from_x(k):
        if k == 3:
            idx = lax.rem(z + 4 - 4 * core, RING)
        else:
            idx = lax.rem(z - s_w * (k + 1) + RING, RING)
        idx = (1 - xl) * RING + idx
        for c in xc[k]:
            c.wait_recv()
        sc.append(send(wg.at[idx], wg.at[idx], ss_sem.at[3 + k], sr_sem.at[3 + k], sibling))

    cut = 128
    keep = slice(0, cut)
    rest = slice(cut, text_ref.shape[0])
    back = (r, lax.rem(t + tp_size - 1, tp_size))
    across = (r, lax.rem(xl * RING + lax.rem(z + 3, RING) + 4, tp_size))

    def window(k):
        if k > 0:
            for c in hc[-2:] if k < 5 else hc[-1:]:
                c.wait_recv()
        if k < 4:
            hc.append(send(win.at[k, keep], win.at[k + 1, keep], hs_sem.at[k], hr_sem.at[k], after))
        if k == 0:
            src, dst, dev = win.at[0, rest], relay, column(-3)
        elif k == 1:
            src, dst, dev = relay, win.at[4, rest], across
        elif k < 5:
            src, dst, dev = win.at[6 - k, rest], win.at[5 - k, rest], back
        if k < 5:
            hc.append(send(src, dst, hs_sem.at[4 + k], hr_sem.at[4 + k], dev))

    def serve(point):
        for name in PLAN.get(point, "").split():
            act = {"z": from_column, "y": from_y, "x": to_x, "f": from_x, "h": window}[name[0]]
            act(int(name[1:]))

    serve("S")

    def mlp(pair, which):
        x = xg[2 * pair:2 * pair + 2].reshape(2 * rows, xg.shape[2])
        h = gelu(jnp.dot(x, w1[which], preferred_element_type=jnp.float32)).astype(jnp.bfloat16)
        return jnp.dot(h, w2[which], preferred_element_type=jnp.float32).reshape(2, rows, w2.shape[2])

    for step in range(4):
        for d, s in ((0, 1), (1, -1)):
            rel = -s * (step + 1)
            ag[d, step].wait_recv()
            if step < 3:
                src, dst = xg.at[slot_of(rel)], xg.at[slot_of(rel - s)]
                if step == 2:
                    part = pl.ds(d * half, half)
                    src, dst = src.at[part], dst.at[part]
                ag[d, step + 1] = send(src, dst, as_sem.at[d, step + 1], ar_sem.at[d, step + 1], column(s))
        if step == 0:
            loads[0].wait()
            loads[1].wait()
        pair = (step + 1) % 4
        acc[2 * pair:2 * pair + 2] = mlp(pair, 0)
        if step == 0:
            win[0] = rms_norm(text_ref[...].astype(jnp.float32), dg_ref[...].reshape(1, -1)).astype(jnp.bfloat16)
        serve("A%d" % step)

    fwd = []
    for i, (c, ref) in enumerate(wx):
        c.wait_recv()
        fwd.append(send(ref, ref, fs_sem.at[i], fr_sem.at[i], sibling))
    merge_weights()
    for c in fwd:
        c.wait_recv()

    rs = {}
    for step in range(4):
        pair = (4 - step) % 4
        acc[2 * pair:2 * pair + 2] = acc[2 * pair:2 * pair + 2] + mlp(pair, 1)
        for d, s in ((0, 1), (1, -1)):
            block = acc.at[slot_of(s * (4 - step))]
            out = rs_out.at[d, step]
            if step == 0:
                part = pl.ds(d * half, half)
                out[part] = block[part].astype(jnp.bfloat16)
                rs[d, 0] = send(out.at[part], rs_in.at[d, 0, part], rs_sem.at[d, 0], rr_sem.at[d, 0], column(s))
                continue
            rs[d, step - 1].wait_recv()
            if step == 1:
                part = pl.ds(d * half, half)
                block[part] = block[part] + rs_in[d, 0, part].astype(jnp.float32)
                out[...] = block[...].astype(jnp.bfloat16)
            else:
                out[...] = (block[...] + rs_in[d, step - 1].astype(jnp.float32)).astype(jnp.bfloat16)
            rs[d, step] = send(out, rs_in.at[d, step], rs_sem.at[d, step], rr_sem.at[d, step], column(s))
        if step == 1:
            mf = []
            for i, (c, ref) in enumerate(mx):
                c.wait_recv()
                mf.append(send(ref, ref, ns_sem.at[i], nr_sem.at[i], sibling))
        serve("R%d" % step)
    rs[0, 3].wait_recv()
    rs[1, 3].wait_recv()
    summed = acc[0] + rs_in[0, 3].astype(jnp.float32) + rs_in[1, 3].astype(jnp.float32)
    nrm = layer_norm(patch_ref[...].astype(jnp.float32) + summed, mg_ref[...].reshape(1, -1)).astype(jnp.bfloat16)

    serve("L")
    mrows = rows // 4
    width = wm_hbm.shape[0]
    to_row = lax.broadcasted_iota(jnp.int32, (rows, rows), 0)
    from_row = lax.broadcasted_iota(jnp.int32, (rows, rows), 1)
    order = (4 * (to_row % mrows) + to_row // mrows == from_row).astype(jnp.bfloat16)
    nrm = jnp.dot(order, nrm, preferred_element_type=jnp.float32).astype(jnp.bfloat16)
    for p in range(4):
        line = nrm[p * mrows:(p + 1) * mrows]
        for c in range(4):
            j = 4 * p + c
            fsend[j % RING, j // RING] = line[:, c * width:(c + 1) * width]
    a2a = []
    for k in range(1, RING):
        dest = lax.rem(z + k, RING)
        a2a.append(send(fsend.at[dest], frx.at[RING - k], ts_sem.at[k], tr_sem.at[k], column(k)))
    frx[0] = fsend[z]
    serve("T")
    loads[2].wait()
    for c in mf:
        c.wait_recv()
    for c in a2a:
        c.wait_recv()

    part = jnp.dot(frx[:, 0].reshape(RING * mrows, width), wm[0], preferred_element_type=jnp.float32)
    part = part + jnp.dot(frx[:, 1].reshape(RING * mrows, width), wm[1], preferred_element_type=jnp.float32)
    psend[...] = part.reshape(psend.shape).astype(jnp.bfloat16)
    red = []
    for k in range(1, RING):
        red.append(send(psend.at[k], prx.at[RING - k], ps_sem.at[k], pr_sem.at[k], column(k)))
    serve("M")
    summed = part[:mrows]
    for c in red:
        c.wait_recv()
    for k in range(1, RING):
        summed = summed + prx[k].astype(jnp.float32)
    mine[...] = summed.astype(jnp.bfloat16)

    quad, lane4 = t // 4, lax.rem(t, 4)
    gat = []
    for i in range(2):
        for k in range(4):
            dest = lax.rem(quad + 2 + i, 4) * 4 + lax.rem(lane4 + k, 4)
            gat.append(send(mine, mg.at[t], gs_sem.at[4 * i + k], gr_sem.at[4 * i + k], (r, dest)))
    serve("G")

    seq = text_ref.shape[0]
    depth = wg.shape[1] // 2
    row = lax.broadcasted_iota(jnp.int32, (seq, seq), 0)
    col = lax.broadcasted_iota(jnp.int32, (seq, seq), 1)
    for k in range(tp_size):
        doc[k:k + 1] = doc_ref[:, k * seq:(k + 1) * seq].astype(jnp.float32)
    own = doc[pl.ds(t, 1), :]
    own = jnp.sum(jnp.where(row == col, own, 0.0), axis=1, keepdims=True)
    for k in range(5):
        theirs = doc[pl.ds(lax.rem(t - k + tp_size, tp_size), 1), :]
        kpos = (t - k) * seq + col
        allowed = (kpos >= 0) & (kpos <= t * seq + row) & (theirs == own)
        bias[:, k * seq:(k + 1) * seq] = jnp.where(allowed, 0.0, -1e30)
    serve("D0")
    for c in sc[:3]:
        c.wait_recv()
    for c in hc:
        c.wait_send()
    for c in gat:
        c.wait_recv()
    raw = mg[...].reshape(tp_size * mrows, mg.shape[2])
    image = rms_norm(raw.astype(jnp.float32), dg_ref[...].reshape(1, -1)).astype(jnp.bfloat16)
    for k in range(5):
        pos = (t - k) * seq + lax.broadcasted_iota(jnp.int32, (seq, 1), 0)
        onehot = (pos == slot_ref[...]).astype(jnp.float32)
        hit = jnp.max(onehot, axis=1, keepdims=True) > 0.0
        onehot = onehot.astype(jnp.bfloat16)
        placed = jnp.dot(onehot, image, preferred_element_type=jnp.float32)
        win[k] = jnp.where(hit, placed, win[k].astype(jnp.float32)).astype(jnp.bfloat16)
        if k == 0:
            placed = jnp.dot(onehot, raw, preferred_element_type=jnp.float32)
            total[...] = jnp.where(hit, placed, text_ref[...].astype(jnp.float32))

    lane = lax.broadcasted_iota(jnp.int32, (seq, depth), 1)
    split = depth // 2

    def decode(side, *pairs):
        heads = []
        for p in pairs:
            heads.append(side * RING + lax.rem(z + p, RING))
            heads.append(side * RING + lax.rem(z + RING - p + (4 if p == 0 else 0), RING))
        x = win[...].reshape(5 * seq, win.shape[2])
        first = win[0]
        kvs = [
            lax.dot_general(x, wg[h, :depth], NT, preferred_element_type=jnp.float32).astype(jnp.bfloat16)
            for h in heads
        ]
        qs = [lax.dot_general(first, wg[h, depth:], NT, preferred_element_type=jnp.float32) for h in heads]
        qs = [jnp.where(lane < split, q, 0.0).astype(jnp.bfloat16) for q in qs]
        scores = [
            lax.dot_general(q, kv, NT, preferred_element_type=jnp.float32) * (1.0 / math.sqrt(HD)) + bias[...]
            for q, kv in zip(qs, kvs)
        ]
        raised = [jnp.exp(s - jnp.max(s, axis=1, keepdims=True)) for s in scores]
        mass = [jnp.sum(e, axis=1, keepdims=True) for e in raised]
        mixed = [
            (jnp.dot(e.astype(jnp.bfloat16), kv, preferred_element_type=jnp.float32) / m)[:, split:]
            for e, kv, m in zip(raised, kvs, mass)
        ]
        outs = jnp.concatenate([wg[h, depth + split:] for h in heads], axis=0)
        mixed = jnp.concatenate(mixed, axis=1).astype(jnp.bfloat16)
        total[...] += jnp.dot(mixed, outs, preferred_element_type=jnp.float32)

    decode(xl, 0, 1)
    serve("D1")
    decode(xl, 2, 3)
    serve("D2")
    for c in sc[3:5]:
        c.wait_recv()
    decode(1 - xl, 1, 2)
    serve("D3")
    for c in sc[5:]:
        c.wait_recv()
    decode(1 - xl, 3, 0)
    out_ref[...] = total[...].astype(jnp.bfloat16)
    for c in pending:
        if not any(c is d for d in hc):
            c.wait_send()


NT = (((1,), (1,)), ((), ()))


def block(patches, text, vg, mgain, dgain, slots, docs, wq, wo, w1, w2, wm):
    rows, width = patches.shape
    seq = text.shape[0]
    hidden = w1.shape[1]
    mrows = rows // 4
    bf, f32 = jnp.bfloat16, jnp.float32
    dma = pltpu.SemaphoreType.DMA
    vmem = pl.BlockSpec(memory_space=pltpu.VMEM)
    hbm = pl.BlockSpec(memory_space=pl.ANY)
    return pl.pallas_call(
        vision_kernel,
        out_shape=jax.ShapeDtypeStruct((seq, width), bf),
        in_specs=[vmem] * 9 + [hbm] * 3,
        out_specs=vmem,
        scratch_shapes=[
            pltpu.VMEM((5, seq, width), bf),
            pltpu.VMEM((seq - 128, width), bf),
            pltpu.VMEM((16, seq), f32),
            pltpu.VMEM((16, 4 * 112, width), bf),
            pltpu.VMEM((seq, 5 * seq), f32),
            pltpu.VMEM((seq, width), f32),
            pltpu.VMEM((8, rows, width), bf),
            pltpu.VMEM((8, rows, width), f32),
            pltpu.VMEM((2, width, hidden), bf),
            pltpu.VMEM((2, hidden, width), bf),
            pltpu.VMEM((2, wm.shape[0], width), bf),
            pltpu.VMEM((2, 4, rows, width), bf),
            pltpu.VMEM((2, 4, rows, width), bf),
            pltpu.VMEM((8, 2, mrows, wm.shape[0]), bf),
            pltpu.VMEM((8, 2, mrows, wm.shape[0]), bf),
            pltpu.VMEM((8, mrows, width), bf),
            pltpu.VMEM((8, mrows, width), bf),
            pltpu.VMEM((16, mrows, width), bf),
            pltpu.VMEM((mrows, width), bf),
            dma((4,)), dma((4,)), dma((4,)), dma((4,)), dma((4,)),
            dma((2, 4)), dma((2, 4)), dma((2, 4)), dma((2, 4)),
            dma((8,)), dma((8,)), dma((8,)), dma((8,)), dma((8,)), dma((8,)),
            dma((2,)), dma((2,)), dma((2,)), dma((2,)),
            dma((4,)), dma((4,)), dma((4, 2)), dma((4, 2)), dma((4,)), dma((4,)),
            dma((4, 2)), dma((4, 2)), dma((7,)), dma((7,)), dma((9,)), dma((9,)),
        ],
        compiler_params=pltpu.CompilerParams(
            collective_id=0, has_side_effects=True, vmem_limit_bytes=62 * 2**20
        ),
        name="block",
    )(patches, text, vg, mgain, dgain, slots, docs, wq, wo, w1, w2, wm)


def shards(
    patches, vis_gain, w_fc1, w_fc2, merge_gain, w_merge, slots, text, docs, dec_gain, w_qkv, w_out
):
    text_rows = text[0]
    out = block(
        patches[0], text_rows, vis_gain, merge_gain, dec_gain, slots, docs, w_qkv.T, w_out,
        w_fc1, w_fc2, w_merge,
    )
    return out[None]


def solution(mesh):
    placed = (
        P("req", "tp", None),
        P(),
        P(None, "tp"),
        P("tp", None),
        P(),
        P("tp", None),
        P("req", None),
        P("req", "tp", None),
        P("req", None),
        P(),
        P(None, "tp"),
        P("tp", None),
    )
    return jax.shard_map(
        shards, mesh=mesh, in_specs=placed, out_specs=P("req", "tp", None), check_vma=False
    )
```

```python
import functools
import math

import jax
import jax.numpy as jnp
from jax import lax
from jax.experimental import pallas as pl
from jax.experimental.pallas import tpu as pltpu
from jax.sharding import PartitionSpec as P

HD = 104
EPSILON = 1e-06
PLAN = {
    "A1": "z-1", "A2": "z0", "A3": "z1 h0", "R0": "z2 y0", "R1": "z3", "R2": "y1 x0 h1", "R3": "y2", "L": "x1 h2",
    "T": "y3", "M": "x2 h3", "G": "x3 f0 h4", "D0": "h5", "D1": "f1", "D2": "f2", "D3": "f3",
}
MESH = pl.DeviceIdType.MESH
RING = 8


def layer_norm(values, gains):
    average = jnp.mean(values, axis=-1, keepdims=True)
    centred = values - average
    variance = jnp.mean(centred * centred, axis=-1, keepdims=True)
    return centred * lax.rsqrt(variance + EPSILON) * gains


def rms_norm(values, gains):
    return values * lax.rsqrt(jnp.mean(values * values, axis=-1, keepdims=True) + EPSILON) * gains


def gelu(v):
    return 0.5 * v * (1.0 + lax.erf(v * math.sqrt(0.5)))


def slot_of(rel):
    if rel == 0:
        return 0
    if abs(rel) == 4:
        return 1
    return 2 * abs(rel) + (1 if rel > 0 else 0)


def vision_kernel(
    patch_ref, text_ref, vg_ref, mg_ref, dg_ref, slot_ref, doc_ref, wq_ref, wo_ref, w1_hbm, w2_hbm, wm_hbm,
    out_ref,
    win, relay, doc, wg, bias, total, xg, acc, w1, w2, wm, rs_out, rs_in, fsend, frx, psend, prx, mg, mine,
    local_sem, ws_sem, wr_sem, fs_sem, fr_sem, as_sem, ar_sem, rs_sem, rr_sem,
    ts_sem, tr_sem, ps_sem, pr_sem, gs_sem, gr_sem,
    ms_sem, mr_sem, ns_sem, nr_sem, zs_sem, zr_sem, ys_sem, yr_sem, y2s_sem, y2r_sem, os_sem, or_sem, ss_sem, sr_sem, hs_sem, hr_sem,
):
    r = lax.axis_index("req")
    t = lax.axis_index("tp")
    z = lax.rem(t, RING)
    xl = t // RING
    core = lax.rem(r, 2)
    xhi = lax.rem(r // 2, 2)
    inner = (r, (1 - xl) * RING + z)
    outer = (r + 2 - 4 * xhi, (1 - xl) * RING + z)
    sibling = (r + 1 - 2 * core, t)

    tp_size = 2 * RING
    after = (r, lax.rem(t + 1, tp_size))
    y_next, y_prev = (lax.rem(r + 4, 16), t), (lax.rem(r + 12, 16), t)

    def column(k):
        return (r, xl * RING + lax.rem(z + k + RING, RING))

    rows = patch_ref.shape[0]
    half = rows // 2

    def remote(src, dst, ssem, rsem, dev):
        return pltpu.make_async_remote_copy(
            src_ref=src, dst_ref=dst, send_sem=ssem, recv_sem=rsem, device_id=dev, device_id_type=MESH
        )

    pending = []

    def send(src, dst, ssem, rsem, dev):
        c = remote(src, dst, ssem, rsem, dev)
        c.start()
        pending.append(c)
        return c

    mg[...] = jnp.zeros_like(mg)
    barrier = pltpu.get_barrier_semaphore()
    peers = [(r, lax.rem(t + k, tp_size)) for k in range(1, tp_size)] + [outer, sibling, y_next, y_prev]
    for dev in peers:
        pl.semaphore_signal(barrier, inc=1, device_id=dev, device_id_type=MESH)

    loads = [
        pltpu.make_async_copy(w1_hbm, w1.at[0], local_sem.at[0]),
        pltpu.make_async_copy(w2_hbm, w2.at[0], local_sem.at[1]),
        pltpu.make_async_copy(wm_hbm, wm.at[xl], local_sem.at[2]),
    ]
    for c in loads:
        c.start()

    wide = patch_ref[...].astype(jnp.float32)
    xg[0] = layer_norm(wide, vg_ref[...].reshape(1, -1)).astype(jnp.bfloat16)
    pl.semaphore_wait(barrier, len(peers))

    ag = {}
    for d, s in ((0, 1), (1, -1)):
        ag[d, 0] = send(xg.at[0], xg.at[slot_of(-s)], as_sem.at[d, 0], ar_sem.at[d, 0], column(s))

    n1 = w1_hbm.shape[0] // 4
    n2 = w2_hbm.shape[0] // 4
    wx = []
    for i, dev in ((0, inner), (1, outer)):
        q = core * 2 + i
        a1 = pl.ds(pl.multiple_of(q * n1, 16), n1)
        a2 = pl.ds(pl.multiple_of(q * n2, 16), n2)
        wx.append((send(w1_hbm.at[a1], w1.at[1, a1], ws_sem.at[2 * i], wr_sem.at[2 * i], dev), w1.at[1, a1]))
        wx.append((send(w2_hbm.at[a2], w2.at[1, a2], ws_sem.at[2 * i + 1], wr_sem.at[2 * i + 1], dev), w2.at[1, a2]))
    quarter = wg.shape[1] // 4
    y = r // 4
    s_w = 1 - 2 * core
    ahead = column(s_w)

    def quarter_at(k):
        return pl.ds(pl.multiple_of(lax.rem(y + k, 4) * quarter, 16), quarter)

    def shard_at(k):
        return xl * RING + lax.rem(z - s_w * (k + 1) + RING, RING)

    mx = []

    def merge_weights():
        for i, dev in ((0, inner), (1, outer)):
            at = pl.ds(pl.multiple_of(core * 208 + 112 * i, 16), (112, 96)[i])
            mx.append((send(wm_hbm.at[at], wm.at[xl, at], ms_sem.at[i], mr_sem.at[i], dev), wm.at[1 - xl, at]))

    row = lax.broadcasted_iota(jnp.int32, (3 * quarter, 3 * HD), 0)
    col = lax.broadcasted_iota(jnp.int32, (3 * quarter, 3 * HD), 1)
    second = (row >= quarter).astype(jnp.int32)
    third = (row >= 2 * quarter).astype(jnp.int32)
    inside = row - quarter * (second + third)
    pick = (col == inside + HD * (1 + second - 2 * third)) & (inside < HD)
    pick = pick.astype(jnp.float32).astype(jnp.bfloat16)
    wg[t, :3 * quarter] = jnp.dot(pick, wq_ref[...], preferred_element_type=jnp.float32).astype(jnp.bfloat16)
    row = lax.broadcasted_iota(jnp.int32, (quarter, HD), 0)
    col = lax.broadcasted_iota(jnp.int32, (quarter, HD), 1)
    pick = (row == col).astype(jnp.float32).astype(jnp.bfloat16)
    wg[t, 3 * quarter:] = jnp.dot(pick, wo_ref[...], preferred_element_type=jnp.float32).astype(jnp.bfloat16)

    zc = []
    yc, y2c, xc, sc, hc = {}, {}, {}, [], []

    def from_column(k):
        if k < 0:
            zc.append(send(wg.at[t, quarter_at(0)], wg.at[t, quarter_at(0)], zs_sem.at[0], zr_sem.at[0], ahead))
            return
        piece = wg.at[shard_at(k), quarter_at(0)]
        zc[k].wait_recv()
        if k < 3:
            zc.append(send(piece, piece, zs_sem.at[k + 1], zr_sem.at[k + 1], ahead))
        yc[k] = (
            send(piece, piece, ys_sem.at[k, 0], yr_sem.at[k, 0], y_next),
            send(piece, piece, ys_sem.at[k, 1], yr_sem.at[k, 1], y_prev),
        )

    def from_y(k):
        for c in yc[k]:
            c.wait_recv()
        piece = wg.at[shard_at(k), quarter_at(3 if k % 2 == 0 else 1)]
        y2c[k] = send(piece, piece, y2s_sem.at[k], y2r_sem.at[k], y_next if k % 2 == 0 else y_prev)

    def both_halves(ref, i):
        n = wg.shape[1] // 2
        return ref.at[pl.ds(i * n, n)]

    def to_x(k):
        y2c[k].wait_recv()
        if k == 3:
            idx = xl * RING + lax.rem(z + 4 - 4 * core, RING)
        else:
            idx = shard_at(k)
        xc[k] = [
            send(both_halves(wg.at[idx], i), both_halves(wg.at[idx], i), os_sem.at[k, i], or_sem.at[k, i], dev)
            for i, dev in ((0, inner), (1, outer))
        ]
        if k < 3:
            sc.append(send(wg.at[idx], wg.at[idx], ss_sem.at[k], sr_sem.at[k], sibling))

    def from_x(k):
        if k == 3:
            idx = lax.rem(z + 4 - 4 * core, RING)
        else:
            idx = lax.rem(z - s_w * (k + 1) + RING, RING)
        idx = (1 - xl) * RING + idx
        for c in xc[k]:
            c.wait_recv()
        sc.append(send(wg.at[idx], wg.at[idx], ss_sem.at[3 + k], sr_sem.at[3 + k], sibling))

    cut = 128
    keep = slice(0, cut)
    rest = slice(cut, text_ref.shape[0])
    back = (r, lax.rem(t + tp_size - 1, tp_size))
    across = (r, lax.rem(xl * RING + lax.rem(z + 3, RING) + 4, tp_size))

    def window(k):
        if k > 0:
            for c in hc[-2:] if k < 5 else hc[-1:]:
                c.wait_recv()
        if k < 4:
            hc.append(send(win.at[k, keep], win.at[k + 1, keep], hs_sem.at[k], hr_sem.at[k], after))
        if k == 0:
            src, dst, dev = win.at[0, rest], relay, column(-3)
        elif k == 1:
            src, dst, dev = relay, win.at[4, rest], across
        elif k < 5:
            src, dst, dev = win.at[6 - k, rest], win.at[5 - k, rest], back
        if k < 5:
            hc.append(send(src, dst, hs_sem.at[4 + k], hr_sem.at[4 + k], dev))

    def serve(point):
        for name in PLAN.get(point, "").split():
            act = {"z": from_column, "y": from_y, "x": to_x, "f": from_x, "h": window}[name[0]]
            act(int(name[1:]))

    serve("S")

    def mlp(pair, which):
        x = xg[2 * pair:2 * pair + 2].reshape(2 * rows, xg.shape[2])
        h = gelu(jnp.dot(x, w1[which], preferred_element_type=jnp.float32)).astype(jnp.bfloat16)
        return jnp.dot(h, w2[which], preferred_element_type=jnp.float32).reshape(2, rows, w2.shape[2])

    for step in range(4):
        for d, s in ((0, 1), (1, -1)):
            rel = -s * (step + 1)
            ag[d, step].wait_recv()
            if step < 3:
                src, dst = xg.at[slot_of(rel)], xg.at[slot_of(rel - s)]
                if step == 2:
                    part = pl.ds(d * half, half)
                    src, dst = src.at[part], dst.at[part]
                ag[d, step + 1] = send(src, dst, as_sem.at[d, step + 1], ar_sem.at[d, step + 1], column(s))
        if step == 0:
            loads[0].wait()
            loads[1].wait()
        pair = (step + 1) % 4
        acc[2 * pair:2 * pair + 2] = mlp(pair, 0)
        if step == 0:
            win[0] = rms_norm(text_ref[...].astype(jnp.float32), dg_ref[...].reshape(1, -1)).astype(jnp.bfloat16)
        serve("A%d" % step)

    fwd = []
    for i, (c, ref) in enumerate(wx):
        c.wait_recv()
        fwd.append(send(ref, ref, fs_sem.at[i], fr_sem.at[i], sibling))
    merge_weights()
    for c in fwd:
        c.wait_recv()

    rs = {}
    for step in range(4):
        pair = (4 - step) % 4
        acc[2 * pair:2 * pair + 2] = acc[2 * pair:2 * pair + 2] + mlp(pair, 1)
        for d, s in ((0, 1), (1, -1)):
            block = acc.at[slot_of(s * (4 - step))]
            out = rs_out.at[d, step]
            if step == 0:
                part = pl.ds(d * half, half)
                out[part] = block[part].astype(jnp.bfloat16)
                rs[d, 0] = send(out.at[part], rs_in.at[d, 0, part], rs_sem.at[d, 0], rr_sem.at[d, 0], column(s))
                continue
            rs[d, step - 1].wait_recv()
            if step == 1:
                part = pl.ds(d * half, half)
                block[part] = block[part] + rs_in[d, 0, part].astype(jnp.float32)
                out[...] = block[...].astype(jnp.bfloat16)
            else:
                out[...] = (block[...] + rs_in[d, step - 1].astype(jnp.float32)).astype(jnp.bfloat16)
            rs[d, step] = send(out, rs_in.at[d, step], rs_sem.at[d, step], rr_sem.at[d, step], column(s))
        if step == 1:
            mf = []
            for i, (c, ref) in enumerate(mx):
                c.wait_recv()
                mf.append(send(ref, ref, ns_sem.at[i], nr_sem.at[i], sibling))
        serve("R%d" % step)
    rs[0, 3].wait_recv()
    rs[1, 3].wait_recv()
    summed = acc[0] + rs_in[0, 3].astype(jnp.float32) + rs_in[1, 3].astype(jnp.float32)
    nrm = layer_norm(patch_ref[...].astype(jnp.float32) + summed, mg_ref[...].reshape(1, -1)).astype(jnp.bfloat16)

    serve("L")
    mrows = rows // 4
    width = wm_hbm.shape[0]
    to_row = lax.broadcasted_iota(jnp.int32, (rows, rows), 0)
    from_row = lax.broadcasted_iota(jnp.int32, (rows, rows), 1)
    order = (4 * (to_row % mrows) + to_row // mrows == from_row).astype(jnp.bfloat16)
    nrm = jnp.dot(order, nrm, preferred_element_type=jnp.float32).astype(jnp.bfloat16)
    for p in range(4):
        line = nrm[p * mrows:(p + 1) * mrows]
        for c in range(4):
            j = 4 * p + c
            fsend[j % RING, j // RING] = line[:, c * width:(c + 1) * width]
    a2a = []
    for k in range(1, RING):
        dest = lax.rem(z + k, RING)
        a2a.append(send(fsend.at[dest], frx.at[RING - k], ts_sem.at[k], tr_sem.at[k], column(k)))
    frx[0] = fsend[z]
    serve("T")
    loads[2].wait()
    for c in mf:
        c.wait_recv()
    for c in a2a:
        c.wait_recv()

    part = jnp.dot(frx[:, 0].reshape(RING * mrows, width), wm[0], preferred_element_type=jnp.float32)
    part = part + jnp.dot(frx[:, 1].reshape(RING * mrows, width), wm[1], preferred_element_type=jnp.float32)
    psend[...] = part.reshape(psend.shape).astype(jnp.bfloat16)
    red = []
    for k in range(1, RING):
        red.append(send(psend.at[k], prx.at[RING - k], ps_sem.at[k], pr_sem.at[k], column(k)))
    serve("M")
    summed = part[:mrows]
    for c in red:
        c.wait_recv()
    for k in range(1, RING):
        summed = summed + prx[k].astype(jnp.float32)
    mine[...] = summed.astype(jnp.bfloat16)

    quad, lane4 = t // 4, lax.rem(t, 4)
    gat = []
    for i in range(2):
        for k in range(4):
            dest = lax.rem(quad + 2 + i, 4) * 4 + lax.rem(lane4 + k, 4)
            gat.append(send(mine, mg.at[t], gs_sem.at[4 * i + k], gr_sem.at[4 * i + k], (r, dest)))
    serve("G")

    seq = text_ref.shape[0]
    depth = wg.shape[1] // 2
    row = lax.broadcasted_iota(jnp.int32, (seq, seq), 0)
    col = lax.broadcasted_iota(jnp.int32, (seq, seq), 1)
    for k in range(tp_size):
        doc[k:k + 1] = doc_ref[:, k * seq:(k + 1) * seq].astype(jnp.float32)
    own = doc[pl.ds(t, 1), :]
    own = jnp.sum(jnp.where(row == col, own, 0.0), axis=1, keepdims=True)
    for k in range(5):
        theirs = doc[pl.ds(lax.rem(t - k + tp_size, tp_size), 1), :]
        kpos = (t - k) * seq + col
        allowed = (kpos >= 0) & (kpos <= t * seq + row) & (theirs == own)
        bias[:, k * seq:(k + 1) * seq] = jnp.where(allowed, 0.0, -1e30)
    serve("D0")
    for c in sc[:3]:
        c.wait_recv()
    for c in hc:
        c.wait_send()
    for c in gat:
        c.wait_recv()
    raw = mg[...].reshape(tp_size * mrows, mg.shape[2])
    image = rms_norm(raw.astype(jnp.float32), dg_ref[...].reshape(1, -1)).astype(jnp.bfloat16)
    for k in range(5):
        pos = (t - k) * seq + lax.broadcasted_iota(jnp.int32, (seq, 1), 0)
        onehot = (pos == slot_ref[...]).astype(jnp.float32)
        hit = jnp.max(onehot, axis=1, keepdims=True) > 0.0
        onehot = onehot.astype(jnp.bfloat16)
        placed = jnp.dot(onehot, image, preferred_element_type=jnp.float32)
        win[k] = jnp.where(hit, placed, win[k].astype(jnp.float32)).astype(jnp.bfloat16)
        if k == 0:
            placed = jnp.dot(onehot, raw, preferred_element_type=jnp.float32)
            total[...] = jnp.where(hit, placed, text_ref[...].astype(jnp.float32))

    lane = lax.broadcasted_iota(jnp.int32, (seq, depth), 1)
    split = depth // 2

    def decode(side, *pairs):
        heads = []
        for p in pairs:
            heads.append(side * RING + lax.rem(z + p, RING))
            heads.append(side * RING + lax.rem(z + RING - p + (4 if p == 0 else 0), RING))
        x = win[...].reshape(5 * seq, win.shape[2])
        first = win[0]
        kvs = [
            lax.dot_general(x, wg[h, :depth], NT, preferred_element_type=jnp.float32).astype(jnp.bfloat16)
            for h in heads
        ]
        qs = [lax.dot_general(first, wg[h, depth:], NT, preferred_element_type=jnp.float32) for h in heads]
        qs = [jnp.where(lane < split, q, 0.0).astype(jnp.bfloat16) for q in qs]
        scores = [
            lax.dot_general(q, kv, NT, preferred_element_type=jnp.float32) * (1.0 / math.sqrt(HD)) + bias[...]
            for q, kv in zip(qs, kvs)
        ]
        raised = [jnp.exp(s - jnp.max(s, axis=1, keepdims=True)) for s in scores]
        mass = [jnp.sum(e, axis=1, keepdims=True) for e in raised]
        mixed = [
            (jnp.dot(e.astype(jnp.bfloat16), kv, preferred_element_type=jnp.float32) / m)[:, split:]
            for e, kv, m in zip(raised, kvs, mass)
        ]
        outs = jnp.concatenate([wg[h, depth + split:] for h in heads], axis=0)
        mixed = jnp.concatenate(mixed, axis=1).astype(jnp.bfloat16)
        total[...] += jnp.dot(mixed, outs, preferred_element_type=jnp.float32)

    decode(xl, 0, 1)
    serve("D1")
    decode(xl, 2, 3)
    serve("D2")
    for c in sc[3:5]:
        c.wait_recv()
    decode(1 - xl, 1, 2)
    serve("D3")
    for c in sc[5:]:
        c.wait_recv()
    decode(1 - xl, 3, 0)
    out_ref[...] = total[...].astype(jnp.bfloat16)
    for c in pending:
        if not any(c is d for d in hc):
            c.wait_send()


NT = (((1,), (1,)), ((), ()))


def block(patches, text, vg, mgain, dgain, slots, docs, wq, wo, w1, w2, wm):
    rows, width = patches.shape
    seq = text.shape[0]
    hidden = w1.shape[1]
    mrows = rows // 4
    bf, f32 = jnp.bfloat16, jnp.float32
    dma = pltpu.SemaphoreType.DMA
    vmem = pl.BlockSpec(memory_space=pltpu.VMEM)
    hbm = pl.BlockSpec(memory_space=pl.ANY)
    return pl.pallas_call(
        vision_kernel,
        out_shape=jax.ShapeDtypeStruct((seq, width), bf),
        in_specs=[vmem] * 9 + [hbm] * 3,
        out_specs=vmem,
        scratch_shapes=[
            pltpu.VMEM((5, seq, width), bf),
            pltpu.VMEM((seq - 128, width), bf),
            pltpu.VMEM((16, seq), f32),
            pltpu.VMEM((16, 4 * 112, width), bf),
            pltpu.VMEM((seq, 5 * seq), f32),
            pltpu.VMEM((seq, width), f32),
            pltpu.VMEM((8, rows, width), bf),
            pltpu.VMEM((8, rows, width), f32),
            pltpu.VMEM((2, width, hidden), bf),
            pltpu.VMEM((2, hidden, width), bf),
            pltpu.VMEM((2, wm.shape[0], width), bf),
            pltpu.VMEM((2, 4, rows, width), bf),
            pltpu.VMEM((2, 4, rows, width), bf),
            pltpu.VMEM((8, 2, mrows, wm.shape[0]), bf),
            pltpu.VMEM((8, 2, mrows, wm.shape[0]), bf),
            pltpu.VMEM((8, mrows, width), bf),
            pltpu.VMEM((8, mrows, width), bf),
            pltpu.VMEM((16, mrows, width), bf),
            pltpu.VMEM((mrows, width), bf),
            dma((4,)), dma((4,)), dma((4,)), dma((4,)), dma((4,)),
            dma((2, 4)), dma((2, 4)), dma((2, 4)), dma((2, 4)),
            dma((8,)), dma((8,)), dma((8,)), dma((8,)), dma((8,)), dma((8,)),
            dma((2,)), dma((2,)), dma((2,)), dma((2,)),
            dma((4,)), dma((4,)), dma((4, 2)), dma((4, 2)), dma((4,)), dma((4,)),
            dma((4, 2)), dma((4, 2)), dma((7,)), dma((7,)), dma((9,)), dma((9,)),
        ],
        compiler_params=pltpu.CompilerParams(
            collective_id=0, has_side_effects=True, vmem_limit_bytes=62 * 2**20
        ),
        name="block",
    )(patches, text, vg, mgain, dgain, slots, docs, wq, wo, w1, w2, wm)


def shards(
    patches, vis_gain, w_fc1, w_fc2, merge_gain, w_merge, slots, text, docs, dec_gain, w_qkv, w_out
):
    text_rows = text[0]
    out = block(
        patches[0], text_rows, vis_gain, merge_gain, dec_gain, slots, docs, w_qkv.T, w_out,
        w_fc1, w_fc2, w_merge,
    )
    return out[None]


def solution(mesh):
    placed = (
        P("req", "tp", None),
        P(),
        P(None, "tp"),
        P("tp", None),
        P(),
        P("tp", None),
        P("req", None),
        P("req", "tp", None),
        P("req", None),
        P(),
        P(None, "tp"),
        P("tp", None),
    )
    return jax.shard_map(
        shards, mesh=mesh, in_specs=placed, out_specs=P("req", "tp", None), check_vma=False
    )
```
